256 devices in a mesh: src: 32 (over z, y), tgt: 8 (over x, core).
Axes of the slice: x: 4, y: 4, z: 8, core: 2. Of those that a mesh axis runs over, the one named last changes fastest.
Arguments:
- source: bfloat16 [32768, 300], P('src'), may hold values from -70 to 70
- target: bfloat16 [16384, 300], P('tgt'), may hold values from -11 to 11
- start_map: float32 [300, 300], replicated, may hold values from -1.5 to 1.5
Outputs:
- source_soft: bfloat16 [32768, 300], P(('src', 'tgt'))
- target_soft: bfloat16 [16384, 300], P('tgt')
- polar_map: float32 [300, 300], replicated
The draws below stay inside these ranges and needn't reach their ends.
All inputs are finite; a program needn't handle non-finite values.
Results may differ from the reference program's by a relative error of at most 0.014.
The reference program's roundings to bfloat16 on the way (of `mapped`, `row_weights` and `col_weights`) count: a program that leaves them out, or rounds other values in their place, can miss the bound.
Values may be sent and summed in bfloat16 or wider, within the bound.
A program may use at most 64 MiB of HBM per device.

```python
import math
import jax
import jax.numpy as jnp
from jax import lax

D = 300
SRC_DEV = 1024
ITERS = 2
NEWTON_STEPS = 8
NS = 32768
NT = 16384
N_SRC = 32


def draw_source(key, part):
    values = jnp.clip(jax.random.normal(jax.random.fold_in(key, 1), (NS, D), jnp.float32), -5.0, 5.0)
    scales = jnp.exp(jax.random.uniform(jax.random.fold_in(key, 2), (NS,), jnp.float32, -0.6931472, 0.6931472))
    values = values * scales[:, None]
    return values.astype(jnp.bfloat16)


def draw_target(key, part):
    values = jnp.clip(jax.random.normal(jax.random.fold_in(key, 3), (NT, D), jnp.float32), -5.0, 5.0)
    scales = jnp.exp(jax.random.uniform(jax.random.fold_in(key, 4), (NT,), jnp.float32, -0.6931472, 0.6931472))
    values = values * scales[:, None]
    return values.astype(jnp.bfloat16)


def draw_start_map(key, part):
    diagonal = jax.random.uniform(jax.random.fold_in(key, 5), (D,), jnp.float32, 0.7, 1.3)
    off_part = jnp.clip(jax.random.normal(jax.random.fold_in(key, 6), (D, D), jnp.float32), -4.0, 4.0) * (0.25 / math.sqrt(D))
    return jnp.diag(diagonal) + off_part


def setup_inputs(seed: int = 0) -> dict:
    seeds = jax.random.split(jax.random.key(seed), 4)
    source = draw_source(jax.random.fold_in(seeds[3], 71), 0)
    target = draw_target(jax.random.fold_in(seeds[3], 71), 0)
    start_map = draw_start_map(jax.random.fold_in(seeds[3], 71), 0)
    return dict(source=source, target=target, start_map=start_map)


def polar_steps(covariance):
    highest = lax.Precision.HIGHEST
    current = covariance / jnp.sqrt(jnp.sum(covariance * covariance) + 1e-06)
    for newton in range(NEWTON_STEPS):
        gram_matrix = jnp.dot(current.T, current, precision=highest)
        current = 1.5 * current - 0.5 * jnp.dot(current, gram_matrix, precision=highest)
    return current

def reference(source, target, start_map):
    highest = lax.Precision.HIGHEST
    score_scale = 2.0 / math.sqrt(D)
    current = start_map
    source_blocks = source.reshape(N_SRC, SRC_DEV, D)
    source_soft = jnp.zeros((NS, D), jnp.bfloat16)
    target_soft = jnp.zeros((NT, D), jnp.bfloat16)
    for iteration in range(ITERS):
        mapped = jnp.dot(source, current.astype(jnp.bfloat16), preferred_element_type=jnp.float32).astype(jnp.bfloat16)
        mapped_blocks = mapped.reshape(N_SRC, SRC_DEV, D)

        def block_stats(running, mapped_rows):
            col_top, col_total = running
            scores = jnp.dot(mapped_rows, target.T, preferred_element_type=jnp.float32) * score_scale
            row_top = lax.optimization_barrier(jnp.max(scores, axis=1))
            row_total = lax.optimization_barrier(jnp.sum(jnp.exp(scores - row_top[:, None]), axis=1))
            new_top = jnp.maximum(col_top, lax.optimization_barrier(jnp.max(scores, axis=0)))
            col_total = col_total * jnp.exp(col_top - new_top) + lax.optimization_barrier(jnp.sum(jnp.exp(scores - new_top[None, :]), axis=0))
            return ((new_top, col_total), (row_top, row_total))
        starting = (jnp.full((NT,), -jnp.inf, jnp.float32), jnp.zeros((NT,), jnp.float32))
        (col_top, col_total), (row_tops, row_totals) = lax.scan(block_stats, starting, mapped_blocks)

        def block_weigh(collected, pieces):
            mapped_rows, source_rows, row_top, row_total = pieces
            scores = jnp.dot(mapped_rows, target.T, preferred_element_type=jnp.float32) * score_scale
            row_weights = (jnp.exp(scores - row_top[:, None]) / row_total[:, None]).astype(jnp.bfloat16)
            col_weights = (jnp.exp(scores - col_top[None, :]) / col_total[None, :]).astype(jnp.bfloat16)
            sum_rows = jnp.dot(row_weights, target, preferred_element_type=jnp.float32)
            collected = collected + jnp.dot(col_weights.T, source_rows, preferred_element_type=jnp.float32)
            return (collected, sum_rows)
        target_sum, sum_blocks = lax.scan(block_weigh, jnp.zeros((NT, D), jnp.float32), (mapped_blocks, source_blocks, row_tops, row_totals))
        source_sum = sum_blocks.reshape(NS, D)
        source_soft = source_sum.astype(jnp.bfloat16)
        target_soft = target_sum.astype(jnp.bfloat16)
        covariance = jnp.dot(source.astype(jnp.float32).T, source_sum, precision=highest) + jnp.dot(target_sum.T, target.astype(jnp.float32), precision=highest)
        current = polar_steps(covariance)
    return (source_soft, target_soft, current)
```

```python
import math

import jax
import jax.numpy as jnp
from jax import lax
from jax.sharding import PartitionSpec as P

ITERS = 2
NEWTON_STEPS = 8


def polar_steps(covariance):
    highest = lax.Precision.HIGHEST
    current = covariance / jnp.sqrt(jnp.sum(covariance * covariance) + 1e-06)
    for newton in range(NEWTON_STEPS):
        gram_matrix = jnp.dot(current.T, current, precision=highest)
        current = 1.5 * current - 0.5 * jnp.dot(current, gram_matrix, precision=highest)
    return current


def merge_stats(top, total, axis):
    gathered = lax.all_gather(jnp.stack([top, total]), axis)
    tops, totals = gathered[:, 0], gathered[:, 1]
    best = jnp.max(tops, axis=0)
    return best, jnp.sum(totals * jnp.exp(tops - best[None]), axis=0)


def body(source, target, start_map):
    highest = lax.Precision.HIGHEST
    score_scale = 2.0 / math.sqrt(source.shape[1])
    source_f32 = source.astype(jnp.float32)
    target_f32 = target.astype(jnp.float32)
    current = start_map
    for iteration in range(ITERS):
        mapped = jnp.dot(
            source, current.astype(jnp.bfloat16), preferred_element_type=jnp.float32
        ).astype(jnp.bfloat16)
        scores = (
            lax.dot_general(
                mapped, target, (((1,), (1,)), ((), ())), preferred_element_type=jnp.float32
            )
            * score_scale
        )
        row_local = jnp.max(scores, axis=1)
        col_local = jnp.max(scores, axis=0)
        row_part = jnp.sum(jnp.exp(scores - row_local[:, None]), axis=1)
        col_part = jnp.sum(jnp.exp(scores - col_local[None, :]), axis=0)
        row_top, row_total = merge_stats(row_local, row_part, "tgt")
        col_top, col_total = merge_stats(col_local, col_part, "src")
        row_weights = (jnp.exp(scores - row_top[:, None]) / row_total[:, None]).astype(jnp.bfloat16)
        col_weights = (jnp.exp(scores - col_top[None, :]) / col_total[None, :]).astype(jnp.bfloat16)
        source_part = jnp.dot(row_weights, target, preferred_element_type=jnp.float32)
        target_part = lax.dot_general(
            col_weights, source, (((0,), (0,)), ((), ())), preferred_element_type=jnp.float32
        )
        covariance = jnp.dot(source_f32.T, source_part, precision=highest)
        covariance = covariance + jnp.dot(target_part.T, target_f32, precision=highest)
        covariance = lax.psum(covariance, ("src", "tgt"))
        if iteration == ITERS - 1:
            source_soft = lax.psum_scatter(
                source_part, "tgt", scatter_dimension=0, tiled=True
            ).astype(jnp.bfloat16)
            target_soft = lax.psum(target_part, "src").astype(jnp.bfloat16)
        current = polar_steps(covariance)
    return (source_soft, target_soft, current)


def solution(mesh):
    in_specs = (P("src", None), P("tgt", None), P())
    out_specs = (P(("src", "tgt"), None), P("tgt", None), P())
    return jax.shard_map(body, mesh=mesh, in_specs=in_specs, out_specs=out_specs, check_vma=False)
```

```python
import math

import functools

import jax
import jax.numpy as jnp
from jax import lax
from jax.experimental import pallas as pl
from jax.experimental.pallas import tpu as pltpu
from jax.sharding import PartitionSpec as P

MESH = pl.DeviceIdType.MESH

ITERS = 2
NEWTON_STEPS = 8


def polar_steps(covariance):
    highest = lax.Precision.HIGHEST
    current = covariance / jnp.sqrt(jnp.sum(covariance * covariance) + 1e-06)
    for newton in range(NEWTON_STEPS):
        gram_matrix = jnp.dot(current.T, current, precision=highest)
        current = 1.5 * current - 0.5 * jnp.dot(current, gram_matrix, precision=highest)
    return current


def all_reduce_kernel(n_src, n_tgt, x_ref, out_ref, gather_src, gather_tgt,
                      send_a, recv_a, send_b, recv_b, send_c, recv_c):
    me_s = lax.axis_index("src")
    me_t = lax.axis_index("tgt")

    def copy(src, dst, send, recv, device):
        return pltpu.make_async_remote_copy(
            src_ref=src, dst_ref=dst, send_sem=send, recv_sem=recv,
            device_id=device, device_id_type=MESH)

    def start_a(d, carry):
        k = lax.rem(me_s + d, n_src)
        copy(x_ref.at[k], gather_src.at[me_s], send_a.at[k], recv_a.at[me_s], (k, me_t)).start()
        return carry
    lax.fori_loop(1, n_src, start_a, 0)
    gather_src[me_s] = x_ref[me_s]

    def wait_a(d, carry):
        k = lax.rem(me_s + d, n_src)
        copy(x_ref.at[k], gather_src.at[me_s], send_a.at[k], recv_a.at[me_s], (k, me_t)).wait_send()
        j = lax.rem(me_s + n_src - d, n_src)
        copy(x_ref.at[j], gather_src.at[j], send_a.at[j], recv_a.at[j], (j, me_t)).wait_recv()
        return carry
    lax.fori_loop(1, n_src, wait_a, 0)
    gather_tgt[me_t] = jnp.sum(gather_src[...], axis=0)

    def start_b(d, carry):
        k = lax.rem(me_t + d, n_tgt)
        copy(gather_tgt.at[me_t], gather_tgt.at[me_t], send_b.at[k], recv_b.at[me_t], (me_s, k)).start()
        return carry
    lax.fori_loop(1, n_tgt, start_b, 0)

    def wait_b(d, carry):
        k = lax.rem(me_t + d, n_tgt)
        copy(gather_tgt.at[me_t], gather_tgt.at[me_t], send_b.at[k], recv_b.at[me_t], (me_s, k)).wait_send()
        j = lax.rem(me_t + n_tgt - d, n_tgt)
        copy(gather_tgt.at[j], gather_tgt.at[j], send_b.at[j], recv_b.at[j], (me_s, j)).wait_recv()
        return carry
    lax.fori_loop(1, n_tgt, wait_b, 0)
    out_ref[me_s] = jnp.sum(gather_tgt[...], axis=0)

    def start_c(d, carry):
        k = lax.rem(me_s + d, n_src)
        copy(out_ref.at[me_s], out_ref.at[me_s], send_c.at[k], recv_c.at[me_s], (k, me_t)).start()
        return carry
    lax.fori_loop(1, n_src, start_c, 0)

    def wait_c(d, carry):
        k = lax.rem(me_s + d, n_src)
        copy(out_ref.at[me_s], out_ref.at[me_s], send_c.at[k], recv_c.at[me_s], (k, me_t)).wait_send()
        j = lax.rem(me_s + n_src - d, n_src)
        copy(out_ref.at[j], out_ref.at[j], send_c.at[j], recv_c.at[j], (j, me_t)).wait_recv()
        return carry
    lax.fori_loop(1, n_src, wait_c, 0)


def all_reduce(matrix):
    n_src = lax.axis_size("src")
    n_tgt = lax.axis_size("tgt")
    size = matrix.size
    lines = -(-size // 128)
    rows = -(-lines // (n_src * 8)) * 8
    flat = jnp.pad(matrix.reshape(-1), (0, n_src * rows * 128 - size)).reshape(n_src, rows, 128)
    vmem = pl.BlockSpec(memory_space=pltpu.VMEM)
    out = pl.pallas_call(
        functools.partial(all_reduce_kernel, n_src, n_tgt),
        out_shape=jax.ShapeDtypeStruct(flat.shape, jnp.float32),
        in_specs=[vmem],
        out_specs=vmem,
        scratch_shapes=[
            pltpu.VMEM((n_src, rows, 128), jnp.float32),
            pltpu.VMEM((n_tgt, rows, 128), jnp.float32),
            pltpu.SemaphoreType.DMA((n_src,)),
            pltpu.SemaphoreType.DMA((n_src,)),
            pltpu.SemaphoreType.DMA((n_tgt,)),
            pltpu.SemaphoreType.DMA((n_tgt,)),
            pltpu.SemaphoreType.DMA((n_src,)),
            pltpu.SemaphoreType.DMA((n_src,)),
        ],
        compiler_params=pltpu.CompilerParams(has_side_effects=True),
    )(flat)
    return out.reshape(-1)[:size].reshape(matrix.shape)


def merge_stats(top, total, axis):
    gathered = lax.all_gather(jnp.stack([top, total]), axis)
    tops, totals = gathered[:, 0], gathered[:, 1]
    best = jnp.max(tops, axis=0)
    return best, jnp.sum(totals * jnp.exp(tops - best[None]), axis=0)


def body(source, target, start_map):
    highest = lax.Precision.HIGHEST
    score_scale = 2.0 / math.sqrt(source.shape[1])
    source_f32 = source.astype(jnp.float32)
    target_f32 = target.astype(jnp.float32)
    current = start_map
    for iteration in range(ITERS):
        mapped = jnp.dot(
            source, current.astype(jnp.bfloat16), preferred_element_type=jnp.float32
        ).astype(jnp.bfloat16)
        scores = (
            lax.dot_general(
                mapped, target, (((1,), (1,)), ((), ())), preferred_element_type=jnp.float32
            )
            * score_scale
        )
        row_local = jnp.max(scores, axis=1)
        col_local = jnp.max(scores, axis=0)
        row_part = jnp.sum(jnp.exp(scores - row_local[:, None]), axis=1)
        col_part = jnp.sum(jnp.exp(scores - col_local[None, :]), axis=0)
        row_top, row_total = merge_stats(row_local, row_part, "tgt")
        col_top, col_total = merge_stats(col_local, col_part, "src")
        row_weights = (jnp.exp(scores - row_top[:, None]) / row_total[:, None]).astype(jnp.bfloat16)
        col_weights = (jnp.exp(scores - col_top[None, :]) / col_total[None, :]).astype(jnp.bfloat16)
        source_part = jnp.dot(row_weights, target, preferred_element_type=jnp.float32)
        target_part = lax.dot_general(
            col_weights, source, (((0,), (0,)), ((), ())), preferred_element_type=jnp.float32
        )
        covariance = jnp.dot(source_f32.T, source_part, precision=highest)
        covariance = covariance + jnp.dot(target_part.T, target_f32, precision=highest)
        covariance = all_reduce(covariance)
        if iteration == ITERS - 1:
            source_soft = lax.psum_scatter(
                source_part, "tgt", scatter_dimension=0, tiled=True
            ).astype(jnp.bfloat16)
            target_soft = lax.psum(target_part, "src").astype(jnp.bfloat16)
        current = polar_steps(covariance)
    return (source_soft, target_soft, current)


def solution(mesh):
    in_specs = (P("src", None), P("tgt", None), P())
    out_specs = (P(("src", "tgt"), None), P("tgt", None), P())
    return jax.shard_map(body, mesh=mesh, in_specs=in_specs, out_specs=out_specs, check_vma=False)
```

```python
import math

import functools

import jax
import jax.numpy as jnp
from jax import lax
from jax.experimental import pallas as pl
from jax.experimental.pallas import tpu as pltpu
from jax.sharding import PartitionSpec as P

MESH = pl.DeviceIdType.MESH

ITERS = 2
NEWTON_STEPS = 8


def polar_steps(covariance):
    highest = lax.Precision.HIGHEST
    current = covariance / jnp.sqrt(jnp.sum(covariance * covariance) + 1e-06)
    for newton in range(NEWTON_STEPS):
        gram_matrix = jnp.dot(current.T, current, precision=highest)
        current = 1.5 * current - 0.5 * jnp.dot(current, gram_matrix, precision=highest)
    return current


def all_reduce_kernel(n_src, n_tgt, x_ref, out_ref, gather_src, gather_tgt,
                      send_a, recv_a, send_b, recv_b, send_c, recv_c):
    me_s = lax.axis_index("src")
    me_t = lax.axis_index("tgt")

    def copy(src, dst, send, recv, device):
        return pltpu.make_async_remote_copy(
            src_ref=src, dst_ref=dst, send_sem=send, recv_sem=recv,
            device_id=device, device_id_type=MESH)

    def start_a(d, carry):
        k = lax.rem(me_s + d, n_src)
        copy(x_ref.at[k], gather_src.at[me_s], send_a.at[k], recv_a.at[me_s], (k, me_t)).start()
        return carry
    lax.fori_loop(1, n_src, start_a, 0)
    gather_src[me_s] = x_ref[me_s]

    def wait_a(d, carry):
        k = lax.rem(me_s + d, n_src)
        copy(x_ref.at[k], gather_src.at[me_s], send_a.at[k], recv_a.at[me_s], (k, me_t)).wait_send()
        j = lax.rem(me_s + n_src - d, n_src)
        copy(x_ref.at[j], gather_src.at[j], send_a.at[j], recv_a.at[j], (j, me_t)).wait_recv()
        return carry
    lax.fori_loop(1, n_src, wait_a, 0)
    gather_tgt[me_t] = jnp.sum(gather_src[...], axis=0)

    def start_b(d, carry):
        k = lax.rem(me_t + d, n_tgt)
        copy(gather_tgt.at[me_t], gather_tgt.at[me_t], send_b.at[k], recv_b.at[me_t], (me_s, k)).start()
        return carry
    lax.fori_loop(1, n_tgt, start_b, 0)

    def wait_b(d, carry):
        k = lax.rem(me_t + d, n_tgt)
        copy(gather_tgt.at[me_t], gather_tgt.at[me_t], send_b.at[k], recv_b.at[me_t], (me_s, k)).wait_send()
        j = lax.rem(me_t + n_tgt - d, n_tgt)
        copy(gather_tgt.at[j], gather_tgt.at[j], send_b.at[j], recv_b.at[j], (me_s, j)).wait_recv()
        return carry
    lax.fori_loop(1, n_tgt, wait_b, 0)
    out_ref[me_s] = jnp.sum(gather_tgt[...], axis=0)

    def start_c(d, carry):
        k = lax.rem(me_s + d, n_src)
        copy(out_ref.at[me_s], out_ref.at[me_s], send_c.at[k], recv_c.at[me_s], (k, me_t)).start()
        return carry
    lax.fori_loop(1, n_src, start_c, 0)

    def wait_c(d, carry):
        k = lax.rem(me_s + d, n_src)
        copy(out_ref.at[me_s], out_ref.at[me_s], send_c.at[k], recv_c.at[me_s], (k, me_t)).wait_send()
        j = lax.rem(me_s + n_src - d, n_src)
        copy(out_ref.at[j], out_ref.at[j], send_c.at[j], recv_c.at[j], (j, me_t)).wait_recv()
        return carry
    lax.fori_loop(1, n_src, wait_c, 0)


def all_reduce(matrix):
    n_src = lax.axis_size("src")
    n_tgt = lax.axis_size("tgt")
    size = matrix.size
    lines = -(-size // 128)
    rows = -(-lines // (n_src * 8)) * 8
    flat = jnp.pad(matrix.reshape(-1), (0, n_src * rows * 128 - size)).reshape(n_src, rows, 128)
    vmem = pl.BlockSpec(memory_space=pltpu.VMEM)
    out = pl.pallas_call(
        functools.partial(all_reduce_kernel, n_src, n_tgt),
        out_shape=jax.ShapeDtypeStruct(flat.shape, jnp.float32),
        in_specs=[vmem],
        out_specs=vmem,
        scratch_shapes=[
            pltpu.VMEM((n_src, rows, 128), jnp.float32),
            pltpu.VMEM((n_tgt, rows, 128), jnp.float32),
            pltpu.SemaphoreType.DMA((n_src,)),
            pltpu.SemaphoreType.DMA((n_src,)),
            pltpu.SemaphoreType.DMA((n_tgt,)),
            pltpu.SemaphoreType.DMA((n_tgt,)),
            pltpu.SemaphoreType.DMA((n_src,)),
            pltpu.SemaphoreType.DMA((n_src,)),
        ],
        compiler_params=pltpu.CompilerParams(has_side_effects=True),
    )(flat)
    return out.reshape(-1)[:size].reshape(matrix.shape)


def src_sum_kernel(n_src, x_ref, out_ref, gather, send_a, recv_a, send_c, recv_c):
    me_s = lax.axis_index("src")
    me_t = lax.axis_index("tgt")

    def copy(src, dst, send, recv, device):
        return pltpu.make_async_remote_copy(
            src_ref=src, dst_ref=dst, send_sem=send, recv_sem=recv,
            device_id=device, device_id_type=MESH)

    def start_a(d, carry):
        k = lax.rem(me_s + d, n_src)
        copy(x_ref.at[k], gather.at[me_s], send_a.at[k], recv_a.at[me_s], (k, me_t)).start()
        return carry
    lax.fori_loop(1, n_src, start_a, 0)
    gather[me_s] = x_ref[me_s]

    def wait_a(d, carry):
        k = lax.rem(me_s + d, n_src)
        copy(x_ref.at[k], gather.at[me_s], send_a.at[k], recv_a.at[me_s], (k, me_t)).wait_send()
        j = lax.rem(me_s + n_src - d, n_src)
        copy(x_ref.at[j], gather.at[j], send_a.at[j], recv_a.at[j], (j, me_t)).wait_recv()
        return carry
    lax.fori_loop(1, n_src, wait_a, 0)
    out_ref[me_s] = jnp.sum(gather[...], axis=0).astype(out_ref.dtype)

    def start_c(d, carry):
        k = lax.rem(me_s + d, n_src)
        copy(out_ref.at[me_s], out_ref.at[me_s], send_c.at[k], recv_c.at[me_s], (k, me_t)).start()
        return carry
    lax.fori_loop(1, n_src, start_c, 0)

    def wait_c(d, carry):
        k = lax.rem(me_s + d, n_src)
        copy(out_ref.at[me_s], out_ref.at[me_s], send_c.at[k], recv_c.at[me_s], (k, me_t)).wait_send()
        j = lax.rem(me_s + n_src - d, n_src)
        copy(out_ref.at[j], out_ref.at[j], send_c.at[j], recv_c.at[j], (j, me_t)).wait_recv()
        return carry
    lax.fori_loop(1, n_src, wait_c, 0)


def src_sum(part, dtype):
    n_src = lax.axis_size("src")
    rows, width = part.shape
    chunks = part.reshape(n_src, rows // n_src, width)
    vmem = pl.BlockSpec(memory_space=pltpu.VMEM)
    out = pl.pallas_call(
        functools.partial(src_sum_kernel, n_src),
        out_shape=jax.ShapeDtypeStruct(chunks.shape, dtype),
        in_specs=[vmem],
        out_specs=vmem,
        scratch_shapes=[
            pltpu.VMEM(chunks.shape, jnp.float32),
            pltpu.SemaphoreType.DMA((n_src,)),
            pltpu.SemaphoreType.DMA((n_src,)),
            pltpu.SemaphoreType.DMA((n_src,)),
            pltpu.SemaphoreType.DMA((n_src,)),
        ],
        compiler_params=pltpu.CompilerParams(has_side_effects=True),
    )(chunks)
    return out.reshape(rows, width)


def stats_gather_kernel(n_src, n_tgt, row_ref, col_ref, row_out, col_out,
                        send_r, recv_r, send_c, recv_c):
    me_s = lax.axis_index("src")
    me_t = lax.axis_index("tgt")

    def row_copy(k, slot):
        return pltpu.make_async_remote_copy(
            src_ref=row_ref, dst_ref=row_out.at[slot], send_sem=send_r.at[k],
            recv_sem=recv_r.at[slot], device_id=(me_s, k), device_id_type=MESH)

    def col_copy(k, slot):
        return pltpu.make_async_remote_copy(
            src_ref=col_ref, dst_ref=col_out.at[slot], send_sem=send_c.at[k],
            recv_sem=recv_c.at[slot], device_id=(k, me_t), device_id_type=MESH)

    def start_c(d, carry):
        col_copy(lax.rem(me_s + d, n_src), me_s).start()
        return carry
    lax.fori_loop(1, n_src, start_c, 0)

    def start_r(d, carry):
        row_copy(lax.rem(me_t + d, n_tgt), me_t).start()
        return carry
    lax.fori_loop(1, n_tgt, start_r, 0)
    row_out[me_t] = row_ref[...]
    col_out[me_s] = col_ref[...]

    def wait_r(d, carry):
        row_copy(lax.rem(me_t + d, n_tgt), me_t).wait_send()
        j = lax.rem(me_t + n_tgt - d, n_tgt)
        row_copy(j, j).wait_recv()
        return carry
    lax.fori_loop(1, n_tgt, wait_r, 0)

    def wait_c(d, carry):
        col_copy(lax.rem(me_s + d, n_src), me_s).wait_send()
        j = lax.rem(me_s + n_src - d, n_src)
        col_copy(j, j).wait_recv()
        return carry
    lax.fori_loop(1, n_src, wait_c, 0)


def merge(gathered):
    tops, totals = gathered[:, 0], gathered[:, 1]
    best = jnp.max(tops, axis=0)
    return best, jnp.sum(totals * jnp.exp(tops - best[None]), axis=0)


def gather_stats(row_top, row_part, col_top, col_part):
    n_src = lax.axis_size("src")
    n_tgt = lax.axis_size("tgt")
    n_row, n_col = row_top.shape[0], col_top.shape[0]
    rows = jnp.stack([row_top, row_part]).reshape(2 * n_row // 128, 128)
    cols = jnp.stack([col_top, col_part]).reshape(2 * n_col // 128, 128)
    vmem = pl.BlockSpec(memory_space=pltpu.VMEM)
    row_all, col_all = pl.pallas_call(
        functools.partial(stats_gather_kernel, n_src, n_tgt),
        out_shape=(jax.ShapeDtypeStruct((n_tgt,) + rows.shape, jnp.float32),
                   jax.ShapeDtypeStruct((n_src,) + cols.shape, jnp.float32)),
        in_specs=[vmem, vmem],
        out_specs=(vmem, vmem),
        scratch_shapes=[
            pltpu.SemaphoreType.DMA((n_tgt,)),
            pltpu.SemaphoreType.DMA((n_tgt,)),
            pltpu.SemaphoreType.DMA((n_src,)),
            pltpu.SemaphoreType.DMA((n_src,)),
        ],
        compiler_params=pltpu.CompilerParams(has_side_effects=True),
    )(rows, cols)
    row_top, row_total = merge(row_all.reshape(n_tgt, 2, n_row))
    col_top, col_total = merge(col_all.reshape(n_src, 2, n_col))
    return row_top, row_total, col_top, col_total


def body(source, target, start_map):
    highest = lax.Precision.HIGHEST
    score_scale = 2.0 / math.sqrt(source.shape[1])
    source_f32 = source.astype(jnp.float32)
    target_f32 = target.astype(jnp.float32)
    current = start_map
    for iteration in range(ITERS):
        mapped = jnp.dot(
            source, current.astype(jnp.bfloat16), preferred_element_type=jnp.float32
        ).astype(jnp.bfloat16)
        scores = (
            lax.dot_general(
                mapped, target, (((1,), (1,)), ((), ())), preferred_element_type=jnp.float32
            )
            * score_scale
        )
        row_local = jnp.max(scores, axis=1)
        col_local = jnp.max(scores, axis=0)
        row_part = jnp.sum(jnp.exp(scores - row_local[:, None]), axis=1)
        col_part = jnp.sum(jnp.exp(scores - col_local[None, :]), axis=0)
        row_top, row_total, col_top, col_total = gather_stats(row_local, row_part, col_local, col_part)
        row_weights = (jnp.exp(scores - row_top[:, None]) / row_total[:, None]).astype(jnp.bfloat16)
        col_weights = (jnp.exp(scores - col_top[None, :]) / col_total[None, :]).astype(jnp.bfloat16)
        source_part = jnp.dot(row_weights, target, preferred_element_type=jnp.float32)
        target_part = lax.dot_general(
            col_weights, source, (((0,), (0,)), ((), ())), preferred_element_type=jnp.float32
        )
        covariance = jnp.dot(source_f32.T, source_part, precision=highest)
        covariance = covariance + jnp.dot(target_part.T, target_f32, precision=highest)
        covariance = all_reduce(covariance)
        if iteration == ITERS - 1:
            source_soft = lax.psum_scatter(
                source_part, "tgt", scatter_dimension=0, tiled=True
            ).astype(jnp.bfloat16)
            target_soft = src_sum(target_part, jnp.bfloat16)
        current = polar_steps(covariance)
    return (source_soft, target_soft, current)


def solution(mesh):
    in_specs = (P("src", None), P("tgt", None), P())
    out_specs = (P(("src", "tgt"), None), P("tgt", None), P())
    return jax.shard_map(body, mesh=mesh, in_specs=in_specs, out_specs=out_specs, check_vma=False)
```

```python
import math

import functools

import jax
import jax.numpy as jnp
from jax import lax
from jax.experimental import pallas as pl
from jax.experimental.pallas import tpu as pltpu
from jax.sharding import PartitionSpec as P

MESH = pl.DeviceIdType.MESH

ITERS = 2
NEWTON_STEPS = 8


def polar_steps(covariance):
    highest = lax.Precision.HIGHEST
    current = covariance / jnp.sqrt(jnp.sum(covariance * covariance) + 1e-06)
    for newton in range(NEWTON_STEPS):
        gram_matrix = jnp.dot(current.T, current, precision=highest)
        current = 1.5 * current - 0.5 * jnp.dot(current, gram_matrix, precision=highest)
    return current


def peer_barrier(n_src, n_tgt):
    me_s = lax.axis_index("src")
    me_t = lax.axis_index("tgt")
    barrier = pltpu.get_barrier_semaphore()

    def greet_src(d, carry):
        pl.semaphore_signal(barrier, 1, device_id=(lax.rem(me_s + d, n_src), me_t), device_id_type=MESH)
        return carry
    lax.fori_loop(1, n_src, greet_src, 0)

    def greet_tgt(d, carry):
        pl.semaphore_signal(barrier, 1, device_id=(me_s, lax.rem(me_t + d, n_tgt)), device_id_type=MESH)
        return carry
    lax.fori_loop(1, n_tgt, greet_tgt, 0)
    pl.semaphore_wait(barrier, n_src + n_tgt - 2)


def all_reduce_kernel(n_src, n_tgt, x_ref, out_ref, gather_src, gather_tgt,
                      send_a, recv_a, send_b, recv_b, send_c, recv_c):
    me_s = lax.axis_index("src")
    me_t = lax.axis_index("tgt")
    peer_barrier(n_src, n_tgt)

    def copy(src, dst, send, recv, device):
        return pltpu.make_async_remote_copy(
            src_ref=src, dst_ref=dst, send_sem=send, recv_sem=recv,
            device_id=device, device_id_type=MESH)

    def start_a(d, carry):
        k = lax.rem(me_s + d, n_src)
        copy(x_ref.at[k], gather_src.at[me_s], send_a.at[k], recv_a.at[me_s], (k, me_t)).start()
        return carry
    lax.fori_loop(1, n_src, start_a, 0)
    gather_src[me_s] = x_ref[me_s]

    def wait_a(d, carry):
        k = lax.rem(me_s + d, n_src)
        copy(x_ref.at[k], gather_src.at[me_s], send_a.at[k], recv_a.at[me_s], (k, me_t)).wait_send()
        j = lax.rem(me_s + n_src - d, n_src)
        copy(x_ref.at[j], gather_src.at[j], send_a.at[j], recv_a.at[j], (j, me_t)).wait_recv()
        return carry
    lax.fori_loop(1, n_src, wait_a, 0)
    gather_tgt[me_t] = jnp.sum(gather_src[...], axis=0)

    def start_b(d, carry):
        k = lax.rem(me_t + d, n_tgt)
        copy(gather_tgt.at[me_t], gather_tgt.at[me_t], send_b.at[k], recv_b.at[me_t], (me_s, k)).start()
        return carry
    lax.fori_loop(1, n_tgt, start_b, 0)

    def wait_b(d, carry):
        k = lax.rem(me_t + d, n_tgt)
        copy(gather_tgt.at[me_t], gather_tgt.at[me_t], send_b.at[k], recv_b.at[me_t], (me_s, k)).wait_send()
        j = lax.rem(me_t + n_tgt - d, n_tgt)
        copy(gather_tgt.at[j], gather_tgt.at[j], send_b.at[j], recv_b.at[j], (me_s, j)).wait_recv()
        return carry
    lax.fori_loop(1, n_tgt, wait_b, 0)
    out_ref[me_s] = jnp.sum(gather_tgt[...], axis=0)

    def start_c(d, carry):
        k = lax.rem(me_s + d, n_src)
        copy(out_ref.at[me_s], out_ref.at[me_s], send_c.at[k], recv_c.at[me_s], (k, me_t)).start()
        return carry
    lax.fori_loop(1, n_src, start_c, 0)

    def wait_c(d, carry):
        k = lax.rem(me_s + d, n_src)
        copy(out_ref.at[me_s], out_ref.at[me_s], send_c.at[k], recv_c.at[me_s], (k, me_t)).wait_send()
        j = lax.rem(me_s + n_src - d, n_src)
        copy(out_ref.at[j], out_ref.at[j], send_c.at[j], recv_c.at[j], (j, me_t)).wait_recv()
        return carry
    lax.fori_loop(1, n_src, wait_c, 0)


def all_reduce(matrix):
    n_src = lax.axis_size("src")
    n_tgt = lax.axis_size("tgt")
    size = matrix.size
    lines = -(-size // 128)
    rows = -(-lines // (n_src * 8)) * 8
    flat = jnp.pad(matrix.reshape(-1), (0, n_src * rows * 128 - size)).reshape(n_src, rows, 128)
    vmem = pl.BlockSpec(memory_space=pltpu.VMEM)
    out = pl.pallas_call(
        functools.partial(all_reduce_kernel, n_src, n_tgt),
        out_shape=jax.ShapeDtypeStruct(flat.shape, jnp.float32),
        in_specs=[vmem],
        out_specs=vmem,
        scratch_shapes=[
            pltpu.VMEM((n_src, rows, 128), jnp.float32),
            pltpu.VMEM((n_tgt, rows, 128), jnp.float32),
            pltpu.SemaphoreType.DMA((n_src,)),
            pltpu.SemaphoreType.DMA((n_src,)),
            pltpu.SemaphoreType.DMA((n_tgt,)),
            pltpu.SemaphoreType.DMA((n_tgt,)),
            pltpu.SemaphoreType.DMA((n_src,)),
            pltpu.SemaphoreType.DMA((n_src,)),
        ],
        compiler_params=pltpu.CompilerParams(collective_id=0, has_side_effects=True),
    )(flat)
    return out.reshape(-1)[:size].reshape(matrix.shape)


def src_sum_kernel(n_src, x_ref, out_ref, gather, send_a, recv_a, send_c, recv_c):
    me_s = lax.axis_index("src")
    me_t = lax.axis_index("tgt")
    peer_barrier(n_src, 1)

    def copy(src, dst, send, recv, device):
        return pltpu.make_async_remote_copy(
            src_ref=src, dst_ref=dst, send_sem=send, recv_sem=recv,
            device_id=device, device_id_type=MESH)

    def start_a(d, carry):
        k = lax.rem(me_s + d, n_src)
        copy(x_ref.at[k], gather.at[me_s], send_a.at[k], recv_a.at[me_s], (k, me_t)).start()
        return carry
    lax.fori_loop(1, n_src, start_a, 0)
    gather[me_s] = x_ref[me_s]

    def wait_a(d, carry):
        k = lax.rem(me_s + d, n_src)
        copy(x_ref.at[k], gather.at[me_s], send_a.at[k], recv_a.at[me_s], (k, me_t)).wait_send()
        j = lax.rem(me_s + n_src - d, n_src)
        copy(x_ref.at[j], gather.at[j], send_a.at[j], recv_a.at[j], (j, me_t)).wait_recv()
        return carry
    lax.fori_loop(1, n_src, wait_a, 0)
    out_ref[me_s] = jnp.sum(gather[...].astype(jnp.float32), axis=0).astype(out_ref.dtype)

    def start_c(d, carry):
        k = lax.rem(me_s + d, n_src)
        copy(out_ref.at[me_s], out_ref.at[me_s], send_c.at[k], recv_c.at[me_s], (k, me_t)).start()
        return carry
    lax.fori_loop(1, n_src, start_c, 0)

    def wait_c(d, carry):
        k = lax.rem(me_s + d, n_src)
        copy(out_ref.at[me_s], out_ref.at[me_s], send_c.at[k], recv_c.at[me_s], (k, me_t)).wait_send()
        j = lax.rem(me_s + n_src - d, n_src)
        copy(out_ref.at[j], out_ref.at[j], send_c.at[j], recv_c.at[j], (j, me_t)).wait_recv()
        return carry
    lax.fori_loop(1, n_src, wait_c, 0)


def src_sum(part, dtype):
    n_src = lax.axis_size("src")
    rows, width = part.shape
    chunks = part.astype(jnp.bfloat16).reshape(n_src, rows * width // (n_src * 128), 128)
    vmem = pl.BlockSpec(memory_space=pltpu.VMEM)
    out = pl.pallas_call(
        functools.partial(src_sum_kernel, n_src),
        out_shape=jax.ShapeDtypeStruct(chunks.shape, dtype),
        in_specs=[vmem],
        out_specs=vmem,
        scratch_shapes=[
            pltpu.VMEM(chunks.shape, chunks.dtype),
            pltpu.SemaphoreType.DMA((n_src,)),
            pltpu.SemaphoreType.DMA((n_src,)),
            pltpu.SemaphoreType.DMA((n_src,)),
            pltpu.SemaphoreType.DMA((n_src,)),
        ],
        compiler_params=pltpu.CompilerParams(collective_id=1, has_side_effects=True),
    )(chunks)
    return out.reshape(rows, width)


def stats_gather_kernel(n_src, n_tgt, row_ref, col_ref, row_out, col_out,
                        send_r, recv_r, send_c, recv_c):
    me_s = lax.axis_index("src")
    me_t = lax.axis_index("tgt")
    peer_barrier(n_src, n_tgt)

    def row_copy(k, slot):
        return pltpu.make_async_remote_copy(
            src_ref=row_ref, dst_ref=row_out.at[slot], send_sem=send_r.at[k],
            recv_sem=recv_r.at[slot], device_id=(me_s, k), device_id_type=MESH)

    def col_copy(k, slot):
        return pltpu.make_async_remote_copy(
            src_ref=col_ref, dst_ref=col_out.at[slot], send_sem=send_c.at[k],
            recv_sem=recv_c.at[slot], device_id=(k, me_t), device_id_type=MESH)

    def start_c(d, carry):
        col_copy(lax.rem(me_s + d, n_src), me_s).start()
        return carry
    lax.fori_loop(1, n_src, start_c, 0)

    def start_r(d, carry):
        row_copy(lax.rem(me_t + d, n_tgt), me_t).start()
        return carry
    lax.fori_loop(1, n_tgt, start_r, 0)
    row_out[me_t] = row_ref[...]
    col_out[me_s] = col_ref[...]

    def wait_r(d, carry):
        row_copy(lax.rem(me_t + d, n_tgt), me_t).wait_send()
        j = lax.rem(me_t + n_tgt - d, n_tgt)
        row_copy(j, j).wait_recv()
        return carry
    lax.fori_loop(1, n_tgt, wait_r, 0)

    def wait_c(d, carry):
        col_copy(lax.rem(me_s + d, n_src), me_s).wait_send()
        j = lax.rem(me_s + n_src - d, n_src)
        col_copy(j, j).wait_recv()
        return carry
    lax.fori_loop(1, n_src, wait_c, 0)


def merge(gathered):
    tops, totals = gathered[:, 0], gathered[:, 1]
    best = jnp.max(tops, axis=0)
    return best, jnp.sum(totals * jnp.exp(tops - best[None]), axis=0)


def gather_stats(row_top, row_part, col_top, col_part):
    n_src = lax.axis_size("src")
    n_tgt = lax.axis_size("tgt")
    n_row, n_col = row_top.shape[0], col_top.shape[0]
    rows = jnp.stack([row_top, row_part]).reshape(2 * n_row // 128, 128)
    cols = jnp.stack([col_top, col_part]).reshape(2 * n_col // 128, 128)
    vmem = pl.BlockSpec(memory_space=pltpu.VMEM)
    row_all, col_all = pl.pallas_call(
        functools.partial(stats_gather_kernel, n_src, n_tgt),
        out_shape=(jax.ShapeDtypeStruct((n_tgt,) + rows.shape, jnp.float32),
                   jax.ShapeDtypeStruct((n_src,) + cols.shape, jnp.float32)),
        in_specs=[vmem, vmem],
        out_specs=(vmem, vmem),
        scratch_shapes=[
            pltpu.SemaphoreType.DMA((n_tgt,)),
            pltpu.SemaphoreType.DMA((n_tgt,)),
            pltpu.SemaphoreType.DMA((n_src,)),
            pltpu.SemaphoreType.DMA((n_src,)),
        ],
        compiler_params=pltpu.CompilerParams(collective_id=2, has_side_effects=True),
    )(rows, cols)
    row_top, row_total = merge(row_all.reshape(n_tgt, 2, n_row))
    col_top, col_total = merge(col_all.reshape(n_src, 2, n_col))
    return row_top, row_total, col_top, col_total


def body(source, target, start_map):
    highest = lax.Precision.HIGHEST
    score_scale = 2.0 / math.sqrt(source.shape[1])
    source_f32 = source.astype(jnp.float32)
    target_f32 = target.astype(jnp.float32)
    current = start_map
    for iteration in range(ITERS):
        mapped = jnp.dot(
            source, current.astype(jnp.bfloat16), preferred_element_type=jnp.float32
        ).astype(jnp.bfloat16)
        scores = (
            lax.dot_general(
                mapped, target, (((1,), (1,)), ((), ())), preferred_element_type=jnp.float32
            )
            * score_scale
        )
        row_local = jnp.max(scores, axis=1)
        col_local = jnp.max(scores, axis=0)
        row_part = jnp.sum(jnp.exp(scores - row_local[:, None]), axis=1)
        col_part = jnp.sum(jnp.exp(scores - col_local[None, :]), axis=0)
        row_top, row_total, col_top, col_total = gather_stats(row_local, row_part, col_local, col_part)
        row_weights = (jnp.exp(scores - row_top[:, None]) / row_total[:, None]).astype(jnp.bfloat16)
        col_weights = (jnp.exp(scores - col_top[None, :]) / col_total[None, :]).astype(jnp.bfloat16)
        source_part = jnp.dot(row_weights, target, preferred_element_type=jnp.float32)
        target_part = lax.dot_general(
            col_weights, source, (((0,), (0,)), ((), ())), preferred_element_type=jnp.float32
        )
        covariance = jnp.dot(source_f32.T, source_part, precision=highest)
        covariance = covariance + jnp.dot(target_part.T, target_f32, precision=highest)
        covariance = all_reduce(covariance)
        if iteration == ITERS - 1:
            source_soft = lax.psum_scatter(
                source_part, "tgt", scatter_dimension=0, tiled=True
            ).astype(jnp.bfloat16)
            target_soft = src_sum(target_part, jnp.bfloat16)
        current = polar_steps(covariance)
    return (source_soft, target_soft, current)


def solution(mesh):
    in_specs = (P("src", None), P("tgt", None), P())
    out_specs = (P(("src", "tgt"), None), P("tgt", None), P())
    return jax.shard_map(body, mesh=mesh, in_specs=in_specs, out_specs=out_specs, check_vma=False)
```

```python
import math

import functools

import jax
import jax.numpy as jnp
from jax import lax
from jax.experimental import pallas as pl
from jax.experimental.pallas import tpu as pltpu
from jax.sharding import PartitionSpec as P

MESH = pl.DeviceIdType.MESH

ITERS = 2
NEWTON_STEPS = 8


def polar_steps(covariance):
    highest = lax.Precision.HIGHEST
    current = covariance / jnp.sqrt(jnp.sum(covariance * covariance) + 1e-06)

    def newton(step, current):
        gram_matrix = jnp.dot(current.T, current, precision=highest)
        return 1.5 * current - 0.5 * jnp.dot(current, gram_matrix, precision=highest)
    return lax.fori_loop(0, NEWTON_STEPS, newton, current)


def peer_barrier(n_src, n_tgt):
    me_s = lax.axis_index("src")
    me_t = lax.axis_index("tgt")
    barrier = pltpu.get_barrier_semaphore()

    def greet_src(d, carry):
        pl.semaphore_signal(barrier, 1, device_id=(lax.rem(me_s + d, n_src), me_t), device_id_type=MESH)
        return carry
    lax.fori_loop(1, n_src, greet_src, 0)

    def greet_tgt(d, carry):
        pl.semaphore_signal(barrier, 1, device_id=(me_s, lax.rem(me_t + d, n_tgt)), device_id_type=MESH)
        return carry
    lax.fori_loop(1, n_tgt, greet_tgt, 0)
    pl.semaphore_wait(barrier, n_src + n_tgt - 2)


def remote(src, dst, send, recv, device):
    return pltpu.make_async_remote_copy(
        src_ref=src, dst_ref=dst, send_sem=send, recv_sem=recv,
        device_id=device, device_id_type=MESH)


def start_all(me, n, device, src, slot, send, recv):
    def step(d, carry):
        k = lax.rem(me + d, n)
        remote(src(k), slot(me), send.at[k], recv.at[me], device(k)).start()
        return carry
    lax.fori_loop(1, n, step, 0)


def wait_all(me, n, device, src, slot, send, recv):
    def step(d, carry):
        k = lax.rem(me + d, n)
        remote(src(k), slot(me), send.at[k], recv.at[me], device(k)).wait_send()
        j = lax.rem(me + n - d, n)
        remote(src(j), slot(j), send.at[j], recv.at[j], device(j)).wait_recv()
        return carry
    lax.fori_loop(1, n, step, 0)


def all_reduce_kernel(n_src, n_tgt, with_target, *refs):
    if with_target:
        (xc, xt, oc, ot, gather_src, gather_tgt, gather_t,
         s_a, r_a, s_b, r_b, s_c, r_c, s_ta, r_ta, s_tc, r_tc) = refs
    else:
        xc, oc, gather_src, gather_tgt, s_a, r_a, s_b, r_b, s_c, r_c = refs
    me_s = lax.axis_index("src")
    me_t = lax.axis_index("tgt")
    peer_barrier(n_src, n_tgt)
    on_src = lambda k: (k, me_t)
    on_tgt = lambda k: (me_s, k)

    if with_target:
        start_all(me_s, n_src, on_src, lambda k: xt.at[k], lambda i: gather_t.at[i], s_ta, r_ta)
        gather_t[me_s] = xt[me_s]

    start_all(me_s, n_src, on_src, lambda k: xc.at[k], lambda i: gather_src.at[i], s_a, r_a)
    gather_src[me_s] = xc[me_s]
    wait_all(me_s, n_src, on_src, lambda k: xc.at[k], lambda i: gather_src.at[i], s_a, r_a)
    gather_tgt[me_t] = jnp.sum(gather_src[...], axis=0)

    start_all(me_t, n_tgt, on_tgt, lambda k: gather_tgt.at[me_t], lambda i: gather_tgt.at[i], s_b, r_b)
    wait_all(me_t, n_tgt, on_tgt, lambda k: gather_tgt.at[me_t], lambda i: gather_tgt.at[i], s_b, r_b)
    oc[me_s] = jnp.sum(gather_tgt[...], axis=0)

    start_all(me_s, n_src, on_src, lambda k: oc.at[me_s], lambda i: oc.at[i], s_c, r_c)
    if with_target:
        wait_all(me_s, n_src, on_src, lambda k: xt.at[k], lambda i: gather_t.at[i], s_ta, r_ta)
        ot[me_s] = jnp.sum(gather_t[...].astype(jnp.float32), axis=0).astype(ot.dtype)
        start_all(me_s, n_src, on_src, lambda k: ot.at[me_s], lambda i: ot.at[i], s_tc, r_tc)
    wait_all(me_s, n_src, on_src, lambda k: oc.at[me_s], lambda i: oc.at[i], s_c, r_c)
    if with_target:
        wait_all(me_s, n_src, on_src, lambda k: ot.at[me_s], lambda i: ot.at[i], s_tc, r_tc)


def all_reduce(matrix, target_part=None):
    n_src = lax.axis_size("src")
    n_tgt = lax.axis_size("tgt")
    size = matrix.size
    lines = -(-size // 128)
    rows = -(-lines // (n_src * 8)) * 8
    flat = jnp.pad(matrix.reshape(-1), (0, n_src * rows * 128 - size)).reshape(n_src, rows, 128)
    vmem = pl.BlockSpec(memory_space=pltpu.VMEM)
    sems = [pltpu.SemaphoreType.DMA((n,)) for n in (n_src, n_src, n_tgt, n_tgt, n_src, n_src)]
    scratch = [pltpu.VMEM((n_src, rows, 128), jnp.float32), pltpu.VMEM((n_tgt, rows, 128), jnp.float32)]
    if target_part is None:
        out = pl.pallas_call(
            functools.partial(all_reduce_kernel, n_src, n_tgt, False),
            out_shape=jax.ShapeDtypeStruct(flat.shape, jnp.float32),
            in_specs=[vmem],
            out_specs=vmem,
            scratch_shapes=scratch + sems,
            compiler_params=pltpu.CompilerParams(collective_id=0, has_side_effects=True),
        )(flat)
        return out.reshape(-1)[:size].reshape(matrix.shape)
    t_rows, width = target_part.shape
    chunks = target_part.astype(jnp.bfloat16).reshape(n_src, t_rows * width // (n_src * 128), 128)
    out, target_sum = pl.pallas_call(
        functools.partial(all_reduce_kernel, n_src, n_tgt, True),
        out_shape=(jax.ShapeDtypeStruct(flat.shape, jnp.float32),
                   jax.ShapeDtypeStruct(chunks.shape, jnp.bfloat16)),
        in_specs=[vmem, vmem],
        out_specs=(vmem, vmem),
        scratch_shapes=scratch + [pltpu.VMEM(chunks.shape, jnp.bfloat16)] + sems
        + [pltpu.SemaphoreType.DMA((n_src,)) for _ in range(4)],
        compiler_params=pltpu.CompilerParams(collective_id=1, has_side_effects=True),
    )(flat, chunks)
    return out.reshape(-1)[:size].reshape(matrix.shape), target_sum.reshape(t_rows, width)


def stats_gather_kernel(n_src, n_tgt, row_ref, col_ref, row_out, col_out,
                        send_r, recv_r, send_c, recv_c):
    me_s = lax.axis_index("src")
    me_t = lax.axis_index("tgt")
    peer_barrier(n_src, n_tgt)

    def row_copy(k, slot):
        return pltpu.make_async_remote_copy(
            src_ref=row_ref, dst_ref=row_out.at[slot], send_sem=send_r.at[k],
            recv_sem=recv_r.at[slot], device_id=(me_s, k), device_id_type=MESH)

    def col_copy(k, slot):
        return pltpu.make_async_remote_copy(
            src_ref=col_ref, dst_ref=col_out.at[slot], send_sem=send_c.at[k],
            recv_sem=recv_c.at[slot], device_id=(k, me_t), device_id_type=MESH)

    def start_c(d, carry):
        col_copy(lax.rem(me_s + d, n_src), me_s).start()
        return carry
    lax.fori_loop(1, n_src, start_c, 0)

    def start_r(d, carry):
        row_copy(lax.rem(me_t + d, n_tgt), me_t).start()
        return carry
    lax.fori_loop(1, n_tgt, start_r, 0)
    row_out[me_t] = row_ref[...]
    col_out[me_s] = col_ref[...]

    def wait_r(d, carry):
        row_copy(lax.rem(me_t + d, n_tgt), me_t).wait_send()
        j = lax.rem(me_t + n_tgt - d, n_tgt)
        row_copy(j, j).wait_recv()
        return carry
    lax.fori_loop(1, n_tgt, wait_r, 0)

    def wait_c(d, carry):
        col_copy(lax.rem(me_s + d, n_src), me_s).wait_send()
        j = lax.rem(me_s + n_src - d, n_src)
        col_copy(j, j).wait_recv()
        return carry
    lax.fori_loop(1, n_src, wait_c, 0)


def merge(gathered):
    tops, totals = gathered[:, 0], gathered[:, 1]
    best = jnp.max(tops, axis=0)
    return best, jnp.sum(totals * jnp.exp(tops - best[None]), axis=0)


def gather_stats(row_top, row_part, col_top, col_part):
    n_src = lax.axis_size("src")
    n_tgt = lax.axis_size("tgt")
    n_row, n_col = row_top.shape[0], col_top.shape[0]
    rows = jnp.stack([row_top, row_part]).reshape(2 * n_row // 128, 128)
    cols = jnp.stack([col_top, col_part]).reshape(2 * n_col // 128, 128)
    vmem = pl.BlockSpec(memory_space=pltpu.VMEM)
    row_all, col_all = pl.pallas_call(
        functools.partial(stats_gather_kernel, n_src, n_tgt),
        out_shape=(jax.ShapeDtypeStruct((n_tgt,) + rows.shape, jnp.float32),
                   jax.ShapeDtypeStruct((n_src,) + cols.shape, jnp.float32)),
        in_specs=[vmem, vmem],
        out_specs=(vmem, vmem),
        scratch_shapes=[
            pltpu.SemaphoreType.DMA((n_tgt,)),
            pltpu.SemaphoreType.DMA((n_tgt,)),
            pltpu.SemaphoreType.DMA((n_src,)),
            pltpu.SemaphoreType.DMA((n_src,)),
        ],
        compiler_params=pltpu.CompilerParams(collective_id=2, has_side_effects=True),
    )(rows, cols)
    row_top, row_total = merge(row_all.reshape(n_tgt, 2, n_row))
    col_top, col_total = merge(col_all.reshape(n_src, 2, n_col))
    return row_top, row_total, col_top, col_total


def body(source, target, start_map):
    highest = lax.Precision.HIGHEST
    score_scale = 2.0 / math.sqrt(source.shape[1])
    source_f32 = source.astype(jnp.float32)
    target_f32 = target.astype(jnp.float32)
    current = start_map
    for iteration in range(ITERS):
        mapped = jnp.dot(
            source, current.astype(jnp.bfloat16), preferred_element_type=jnp.float32
        ).astype(jnp.bfloat16)
        scores = (
            lax.dot_general(
                mapped, target, (((1,), (1,)), ((), ())), preferred_element_type=jnp.float32
            )
            * score_scale
        )
        row_local = jnp.max(scores, axis=1)
        col_local = jnp.max(scores, axis=0)
        row_part = jnp.sum(jnp.exp(scores - row_local[:, None]), axis=1)
        col_part = jnp.sum(jnp.exp(scores - col_local[None, :]), axis=0)
        row_top, row_total, col_top, col_total = gather_stats(row_local, row_part, col_local, col_part)
        row_weights = (jnp.exp(scores - row_top[:, None]) / row_total[:, None]).astype(jnp.bfloat16)
        col_weights = (jnp.exp(scores - col_top[None, :]) / col_total[None, :]).astype(jnp.bfloat16)
        source_part = jnp.dot(row_weights, target, preferred_element_type=jnp.float32)
        target_part = lax.dot_general(
            col_weights, source, (((0,), (0,)), ((), ())), preferred_element_type=jnp.float32
        )
        covariance = jnp.dot(source_f32.T, source_part, precision=highest)
        covariance = covariance + jnp.dot(target_part.T, target_f32, precision=highest)
        if iteration == ITERS - 1:
            source_soft = lax.psum_scatter(
                source_part, "tgt", scatter_dimension=0, tiled=True
            ).astype(jnp.bfloat16)
            covariance, target_soft = all_reduce(covariance, target_part)
        else:
            covariance = all_reduce(covariance)
        current = polar_steps(covariance)
    return (source_soft, target_soft, current)


def solution(mesh):
    in_specs = (P("src", None), P("tgt", None), P())
    out_specs = (P(("src", "tgt"), None), P("tgt", None), P())
    return jax.shard_map(body, mesh=mesh, in_specs=in_specs, out_specs=out_specs, check_vma=False)
```

```python
import math

import functools

import jax
import jax.numpy as jnp
from jax import lax
from jax.experimental import pallas as pl
from jax.experimental.pallas import tpu as pltpu
from jax.sharding import PartitionSpec as P

MESH = pl.DeviceIdType.MESH

ITERS = 2
NEWTON_STEPS = 8


def polar_steps(covariance):
    highest = lax.Precision.HIGH
    current = covariance / jnp.sqrt(jnp.sum(covariance * covariance) + 1e-06)

    def newton(step, current):
        gram_matrix = jnp.dot(current.T, current, precision=highest)
        return 1.5 * current - 0.5 * jnp.dot(current, gram_matrix, precision=highest)
    return lax.fori_loop(0, NEWTON_STEPS, newton, current)


def peer_barrier(n_src, n_tgt):
    me_s = lax.axis_index("src")
    me_t = lax.axis_index("tgt")
    barrier = pltpu.get_barrier_semaphore()

    def greet_src(d, carry):
        pl.semaphore_signal(barrier, 1, device_id=(lax.rem(me_s + d, n_src), me_t), device_id_type=MESH)
        return carry
    lax.fori_loop(1, n_src, greet_src, 0)

    def greet_tgt(d, carry):
        pl.semaphore_signal(barrier, 1, device_id=(me_s, lax.rem(me_t + d, n_tgt)), device_id_type=MESH)
        return carry
    lax.fori_loop(1, n_tgt, greet_tgt, 0)
    pl.semaphore_wait(barrier, n_src + n_tgt - 2)


def remote(src, dst, send, recv, device):
    return pltpu.make_async_remote_copy(
        src_ref=src, dst_ref=dst, send_sem=send, recv_sem=recv,
        device_id=device, device_id_type=MESH)


def start_all(me, n, device, src, slot, send, recv):
    def step(d, carry):
        k = lax.rem(me + d, n)
        remote(src(k), slot(me), send.at[k], recv.at[me], device(k)).start()
        return carry
    lax.fori_loop(1, n, step, 0)


def wait_all(me, n, device, src, slot, send, recv):
    def step(d, carry):
        k = lax.rem(me + d, n)
        remote(src(k), slot(me), send.at[k], recv.at[me], device(k)).wait_send()
        j = lax.rem(me + n - d, n)
        remote(src(j), slot(j), send.at[j], recv.at[j], device(j)).wait_recv()
        return carry
    lax.fori_loop(1, n, step, 0)


def all_reduce_kernel(n_src, n_tgt, with_target, *refs):
    if with_target:
        (xc, xt, oc, ot, gather_src, gather_tgt, gather_t,
         s_a, r_a, s_b, r_b, s_c, r_c, s_ta, r_ta, s_tc, r_tc) = refs
    else:
        xc, oc, gather_src, gather_tgt, s_a, r_a, s_b, r_b, s_c, r_c = refs
    me_s = lax.axis_index("src")
    me_t = lax.axis_index("tgt")
    peer_barrier(n_src, n_tgt)
    on_src = lambda k: (k, me_t)
    on_tgt = lambda k: (me_s, k)

    if with_target:
        start_all(me_s, n_src, on_src, lambda k: xt.at[k], lambda i: gather_t.at[i], s_ta, r_ta)
        gather_t[me_s] = xt[me_s]

    start_all(me_s, n_src, on_src, lambda k: xc.at[k], lambda i: gather_src.at[i], s_a, r_a)
    gather_src[me_s] = xc[me_s]
    wait_all(me_s, n_src, on_src, lambda k: xc.at[k], lambda i: gather_src.at[i], s_a, r_a)
    gather_tgt[me_t] = jnp.sum(gather_src[...], axis=0)

    start_all(me_t, n_tgt, on_tgt, lambda k: gather_tgt.at[me_t], lambda i: gather_tgt.at[i], s_b, r_b)
    wait_all(me_t, n_tgt, on_tgt, lambda k: gather_tgt.at[me_t], lambda i: gather_tgt.at[i], s_b, r_b)
    oc[me_s] = jnp.sum(gather_tgt[...], axis=0)

    start_all(me_s, n_src, on_src, lambda k: oc.at[me_s], lambda i: oc.at[i], s_c, r_c)
    if with_target:
        wait_all(me_s, n_src, on_src, lambda k: xt.at[k], lambda i: gather_t.at[i], s_ta, r_ta)
        ot[me_s] = jnp.sum(gather_t[...].astype(jnp.float32), axis=0).astype(ot.dtype)
        start_all(me_s, n_src, on_src, lambda k: ot.at[me_s], lambda i: ot.at[i], s_tc, r_tc)
    wait_all(me_s, n_src, on_src, lambda k: oc.at[me_s], lambda i: oc.at[i], s_c, r_c)
    if with_target:
        wait_all(me_s, n_src, on_src, lambda k: ot.at[me_s], lambda i: ot.at[i], s_tc, r_tc)


def all_reduce(matrix, target_part=None):
    n_src = lax.axis_size("src")
    n_tgt = lax.axis_size("tgt")
    size = matrix.size
    lines = -(-size // 128)
    rows = -(-lines // (n_src * 8)) * 8
    flat = jnp.pad(matrix.reshape(-1), (0, n_src * rows * 128 - size)).reshape(n_src, rows, 128)
    vmem = pl.BlockSpec(memory_space=pltpu.VMEM)
    sems = [pltpu.SemaphoreType.DMA((n,)) for n in (n_src, n_src, n_tgt, n_tgt, n_src, n_src)]
    scratch = [pltpu.VMEM((n_src, rows, 128), jnp.float32), pltpu.VMEM((n_tgt, rows, 128), jnp.float32)]
    if target_part is None:
        out = pl.pallas_call(
            functools.partial(all_reduce_kernel, n_src, n_tgt, False),
            out_shape=jax.ShapeDtypeStruct(flat.shape, jnp.float32),
            in_specs=[vmem],
            out_specs=vmem,
            scratch_shapes=scratch + sems,
            compiler_params=pltpu.CompilerParams(collective_id=0, has_side_effects=True),
        )(flat)
        return out.reshape(-1)[:size].reshape(matrix.shape)
    t_rows, width = target_part.shape
    chunks = target_part.astype(jnp.bfloat16).reshape(n_src, t_rows * width // (n_src * 128), 128)
    out, target_sum = pl.pallas_call(
        functools.partial(all_reduce_kernel, n_src, n_tgt, True),
        out_shape=(jax.ShapeDtypeStruct(flat.shape, jnp.float32),
                   jax.ShapeDtypeStruct(chunks.shape, jnp.bfloat16)),
        in_specs=[vmem, vmem],
        out_specs=(vmem, vmem),
        scratch_shapes=scratch + [pltpu.VMEM(chunks.shape, jnp.bfloat16)] + sems
        + [pltpu.SemaphoreType.DMA((n_src,)) for _ in range(4)],
        compiler_params=pltpu.CompilerParams(collective_id=1, has_side_effects=True),
    )(flat, chunks)
    return out.reshape(-1)[:size].reshape(matrix.shape), target_sum.reshape(t_rows, width)


def stats_gather_kernel(n_src, n_tgt, row_ref, col_ref, row_out, col_out,
                        send_r, recv_r, send_c, recv_c):
    me_s = lax.axis_index("src")
    me_t = lax.axis_index("tgt")
    peer_barrier(n_src, n_tgt)

    def row_copy(k, slot):
        return pltpu.make_async_remote_copy(
            src_ref=row_ref, dst_ref=row_out.at[slot], send_sem=send_r.at[k],
            recv_sem=recv_r.at[slot], device_id=(me_s, k), device_id_type=MESH)

    def col_copy(k, slot):
        return pltpu.make_async_remote_copy(
            src_ref=col_ref, dst_ref=col_out.at[slot], send_sem=send_c.at[k],
            recv_sem=recv_c.at[slot], device_id=(k, me_t), device_id_type=MESH)

    def start_c(d, carry):
        col_copy(lax.rem(me_s + d, n_src), me_s).start()
        return carry
    lax.fori_loop(1, n_src, start_c, 0)

    def start_r(d, carry):
        row_copy(lax.rem(me_t + d, n_tgt), me_t).start()
        return carry
    lax.fori_loop(1, n_tgt, start_r, 0)
    row_out[me_t] = row_ref[...]
    col_out[me_s] = col_ref[...]

    def wait_r(d, carry):
        row_copy(lax.rem(me_t + d, n_tgt), me_t).wait_send()
        j = lax.rem(me_t + n_tgt - d, n_tgt)
        row_copy(j, j).wait_recv()
        return carry
    lax.fori_loop(1, n_tgt, wait_r, 0)

    def wait_c(d, carry):
        col_copy(lax.rem(me_s + d, n_src), me_s).wait_send()
        j = lax.rem(me_s + n_src - d, n_src)
        col_copy(j, j).wait_recv()
        return carry
    lax.fori_loop(1, n_src, wait_c, 0)


def merge(gathered):
    tops, totals = gathered[:, 0], gathered[:, 1]
    best = jnp.max(tops, axis=0)
    return best, jnp.sum(totals * jnp.exp(tops - best[None]), axis=0)


def gather_stats(row_top, row_part, col_top, col_part):
    n_src = lax.axis_size("src")
    n_tgt = lax.axis_size("tgt")
    n_row, n_col = row_top.shape[0], col_top.shape[0]
    rows = jnp.stack([row_top, row_part]).reshape(2 * n_row // 128, 128)
    cols = jnp.stack([col_top, col_part]).reshape(2 * n_col // 128, 128)
    vmem = pl.BlockSpec(memory_space=pltpu.VMEM)
    row_all, col_all = pl.pallas_call(
        functools.partial(stats_gather_kernel, n_src, n_tgt),
        out_shape=(jax.ShapeDtypeStruct((n_tgt,) + rows.shape, jnp.float32),
                   jax.ShapeDtypeStruct((n_src,) + cols.shape, jnp.float32)),
        in_specs=[vmem, vmem],
        out_specs=(vmem, vmem),
        scratch_shapes=[
            pltpu.SemaphoreType.DMA((n_tgt,)),
            pltpu.SemaphoreType.DMA((n_tgt,)),
            pltpu.SemaphoreType.DMA((n_src,)),
            pltpu.SemaphoreType.DMA((n_src,)),
        ],
        compiler_params=pltpu.CompilerParams(collective_id=2, has_side_effects=True),
    )(rows, cols)
    row_top, row_total = merge(row_all.reshape(n_tgt, 2, n_row))
    col_top, col_total = merge(col_all.reshape(n_src, 2, n_col))
    return row_top, row_total, col_top, col_total


def body(source, target, start_map):
    highest = lax.Precision.HIGHEST
    score_scale = 2.0 / math.sqrt(source.shape[1])
    source_f32 = source.astype(jnp.float32)
    target_f32 = target.astype(jnp.float32)
    current = start_map
    for iteration in range(ITERS):
        mapped = jnp.dot(
            source, current.astype(jnp.bfloat16), preferred_element_type=jnp.float32
        ).astype(jnp.bfloat16)
        scores = (
            lax.dot_general(
                mapped, target, (((1,), (1,)), ((), ())), preferred_element_type=jnp.float32
            )
            * score_scale
        )
        row_local = jnp.max(scores, axis=1)
        col_local = jnp.max(scores, axis=0)
        row_part = jnp.sum(jnp.exp(scores - row_local[:, None]), axis=1)
        col_part = jnp.sum(jnp.exp(scores - col_local[None, :]), axis=0)
        row_top, row_total, col_top, col_total = gather_stats(row_local, row_part, col_local, col_part)
        row_weights = (jnp.exp(scores - row_top[:, None]) / row_total[:, None]).astype(jnp.bfloat16)
        col_weights = (jnp.exp(scores - col_top[None, :]) / col_total[None, :]).astype(jnp.bfloat16)
        source_part = jnp.dot(row_weights, target, preferred_element_type=jnp.float32)
        target_part = lax.dot_general(
            col_weights, source, (((0,), (0,)), ((), ())), preferred_element_type=jnp.float32
        )
        covariance = jnp.dot(source_f32.T, source_part, precision=highest)
        covariance = covariance + jnp.dot(target_part.T, target_f32, precision=highest)
        if iteration == ITERS - 1:
            source_soft = lax.psum_scatter(
                source_part, "tgt", scatter_dimension=0, tiled=True
            ).astype(jnp.bfloat16)
            covariance, target_soft = all_reduce(covariance, target_part)
        else:
            covariance = all_reduce(covariance)
        current = polar_steps(covariance)
    return (source_soft, target_soft, current)


def solution(mesh):
    in_specs = (P("src", None), P("tgt", None), P())
    out_specs = (P(("src", "tgt"), None), P("tgt", None), P())
    return jax.shard_map(body, mesh=mesh, in_specs=in_specs, out_specs=out_specs, check_vma=False)
```

```python
import math

import functools

import jax
import jax.numpy as jnp
from jax import lax
from jax.experimental import pallas as pl
from jax.experimental.pallas import tpu as pltpu
from jax.sharding import PartitionSpec as P

MESH = pl.DeviceIdType.MESH

ITERS = 2
NEWTON_STEPS = 8


def polar_steps(covariance):
    highest = lax.Precision.HIGH
    current = covariance / jnp.sqrt(jnp.sum(covariance * covariance) + 1e-06)

    def newton(step, current):
        gram_matrix = jnp.dot(current.T, current, precision=highest)
        return 1.5 * current - 0.5 * jnp.dot(current, gram_matrix, precision=highest)
    return lax.fori_loop(0, NEWTON_STEPS, newton, current)


def peer_barrier(n_src, n_tgt):
    me_s = lax.axis_index("src")
    me_t = lax.axis_index("tgt")
    barrier = pltpu.get_barrier_semaphore()

    def greet_src(d, carry):
        pl.semaphore_signal(barrier, 1, device_id=(lax.rem(me_s + d, n_src), me_t), device_id_type=MESH)
        return carry
    lax.fori_loop(1, n_src, greet_src, 0)

    def greet_tgt(d, carry):
        pl.semaphore_signal(barrier, 1, device_id=(me_s, lax.rem(me_t + d, n_tgt)), device_id_type=MESH)
        return carry
    lax.fori_loop(1, n_tgt, greet_tgt, 0)
    pl.semaphore_wait(barrier, n_src + n_tgt - 2)


def remote(src, dst, send, recv, device):
    return pltpu.make_async_remote_copy(
        src_ref=src, dst_ref=dst, send_sem=send, recv_sem=recv,
        device_id=device, device_id_type=MESH)


def start_all(me, n, device, src, slot, send, recv):
    def step(d, carry):
        k = lax.rem(me + d, n)
        remote(src(k), slot(me), send.at[k], recv.at[me], device(k)).start()
        return carry
    lax.fori_loop(1, n, step, 0)


def wait_all(me, n, device, src, slot, send, recv):
    def step(d, carry):
        k = lax.rem(me + d, n)
        remote(src(k), slot(me), send.at[k], recv.at[me], device(k)).wait_send()
        j = lax.rem(me + n - d, n)
        remote(src(j), slot(j), send.at[j], recv.at[j], device(j)).wait_recv()
        return carry
    lax.fori_loop(1, n, step, 0)


def all_reduce_kernel(n_src, n_tgt, with_target, *refs):
    if with_target:
        (xc, xt, oc, ot, gather_src, gather_tgt, g1, g2, s1,
         s_a, r_a, s_b, r_b, s_c, r_c, s_1, r_1, s_2, r_2, s_3, r_3, s_4, r_4) = refs
    else:
        xc, oc, gather_src, gather_tgt, s_a, r_a, s_b, r_b, s_c, r_c = refs
    me_s = lax.axis_index("src")
    me_t = lax.axis_index("tgt")
    peer_barrier(n_src, n_tgt)
    on_src = lambda k: (k, me_t)
    on_tgt = lambda k: (me_s, k)

    if with_target:
        n_y, n_z = xt.shape[0], xt.shape[1]
        my_z = me_s // n_y
        my_y = me_s % n_y
        on_y = lambda k: (my_z * n_y + k, me_t)
        on_z = lambda k: (k * n_y + my_y, me_t)
        start_all(my_y, n_y, on_y, lambda k: xt.at[k], lambda i: g1.at[i], s_1, r_1)
        g1[my_y] = xt[my_y]

    start_all(me_s, n_src, on_src, lambda k: xc.at[k], lambda i: gather_src.at[i], s_a, r_a)
    gather_src[me_s] = xc[me_s]
    wait_all(me_s, n_src, on_src, lambda k: xc.at[k], lambda i: gather_src.at[i], s_a, r_a)
    gather_tgt[me_t] = jnp.sum(gather_src[...], axis=0)

    if with_target:
        wait_all(my_y, n_y, on_y, lambda k: xt.at[k], lambda i: g1.at[i], s_1, r_1)
        s1[...] = jnp.sum(g1[...].astype(jnp.float32), axis=0).astype(s1.dtype)
        start_all(my_z, n_z, on_z, lambda k: s1.at[k], lambda i: g2.at[i], s_2, r_2)
        g2[my_z] = s1[my_z]

    start_all(me_t, n_tgt, on_tgt, lambda k: gather_tgt.at[me_t], lambda i: gather_tgt.at[i], s_b, r_b)
    wait_all(me_t, n_tgt, on_tgt, lambda k: gather_tgt.at[me_t], lambda i: gather_tgt.at[i], s_b, r_b)
    oc[me_s] = jnp.sum(gather_tgt[...], axis=0)
    start_all(me_s, n_src, on_src, lambda k: oc.at[me_s], lambda i: oc.at[i], s_c, r_c)

    if with_target:
        wait_all(my_z, n_z, on_z, lambda k: s1.at[k], lambda i: g2.at[i], s_2, r_2)
        ot[my_y, my_z] = jnp.sum(g2[...].astype(jnp.float32), axis=0).astype(ot.dtype)
        start_all(my_z, n_z, on_z, lambda k: ot.at[my_y, my_z], lambda i: ot.at[my_y, i], s_3, r_3)
    wait_all(me_s, n_src, on_src, lambda k: oc.at[me_s], lambda i: oc.at[i], s_c, r_c)
    if with_target:
        wait_all(my_z, n_z, on_z, lambda k: ot.at[my_y, my_z], lambda i: ot.at[my_y, i], s_3, r_3)
        start_all(my_y, n_y, on_y, lambda k: ot.at[my_y], lambda i: ot.at[i], s_4, r_4)
        wait_all(my_y, n_y, on_y, lambda k: ot.at[my_y], lambda i: ot.at[i], s_4, r_4)


def all_reduce(matrix, target_part=None):
    n_src = lax.axis_size("src")
    n_tgt = lax.axis_size("tgt")
    size = matrix.size
    lines = -(-size // 128)
    rows = -(-lines // (n_src * 8)) * 8
    flat = jnp.pad(matrix.reshape(-1), (0, n_src * rows * 128 - size)).reshape(n_src, rows, 128)
    vmem = pl.BlockSpec(memory_space=pltpu.VMEM)
    sems = [pltpu.SemaphoreType.DMA((n,)) for n in (n_src, n_src, n_tgt, n_tgt, n_src, n_src)]
    scratch = [pltpu.VMEM((n_src, rows, 128), jnp.float32), pltpu.VMEM((n_tgt, rows, 128), jnp.float32)]
    if target_part is None:
        out = pl.pallas_call(
            functools.partial(all_reduce_kernel, n_src, n_tgt, False),
            out_shape=jax.ShapeDtypeStruct(flat.shape, jnp.float32),
            in_specs=[vmem],
            out_specs=vmem,
            scratch_shapes=scratch + sems,
            compiler_params=pltpu.CompilerParams(collective_id=0, has_side_effects=True),
        )(flat)
        return out.reshape(-1)[:size].reshape(matrix.shape)
    t_rows, width = target_part.shape
    n_y = 4 if n_src % 4 == 0 else n_src
    n_z = n_src // n_y
    lanes = t_rows * width // (n_src * 128)
    chunks = target_part.astype(jnp.bfloat16).reshape(n_z, n_y, lanes, 128).transpose(1, 0, 2, 3)
    out, target_sum = pl.pallas_call(
        functools.partial(all_reduce_kernel, n_src, n_tgt, True),
        out_shape=(jax.ShapeDtypeStruct(flat.shape, jnp.float32),
                   jax.ShapeDtypeStruct(chunks.shape, jnp.bfloat16)),
        in_specs=[vmem, vmem],
        out_specs=(vmem, vmem),
        scratch_shapes=scratch
        + [pltpu.VMEM(chunks.shape, jnp.bfloat16), pltpu.VMEM((n_z, lanes, 128), jnp.bfloat16),
           pltpu.VMEM((n_z, lanes, 128), jnp.bfloat16)]
        + sems
        + [pltpu.SemaphoreType.DMA((n,)) for n in (n_y, n_y, n_z, n_z, n_z, n_z, n_y, n_y)],
        compiler_params=pltpu.CompilerParams(collective_id=1, has_side_effects=True),
    )(flat, chunks)
    target_sum = target_sum.transpose(1, 0, 2, 3).reshape(t_rows, width)
    return out.reshape(-1)[:size].reshape(matrix.shape), target_sum


def stats_gather_kernel(n_src, n_tgt, row_ref, col_ref, row_out, col_out,
                        send_r, recv_r, send_c, recv_c):
    me_s = lax.axis_index("src")
    me_t = lax.axis_index("tgt")
    peer_barrier(n_src, n_tgt)

    def row_copy(k, slot):
        return pltpu.make_async_remote_copy(
            src_ref=row_ref, dst_ref=row_out.at[slot], send_sem=send_r.at[k],
            recv_sem=recv_r.at[slot], device_id=(me_s, k), device_id_type=MESH)

    def col_copy(k, slot):
        return pltpu.make_async_remote_copy(
            src_ref=col_ref, dst_ref=col_out.at[slot], send_sem=send_c.at[k],
            recv_sem=recv_c.at[slot], device_id=(k, me_t), device_id_type=MESH)

    def start_c(d, carry):
        col_copy(lax.rem(me_s + d, n_src), me_s).start()
        return carry
    lax.fori_loop(1, n_src, start_c, 0)

    def start_r(d, carry):
        row_copy(lax.rem(me_t + d, n_tgt), me_t).start()
        return carry
    lax.fori_loop(1, n_tgt, start_r, 0)
    row_out[me_t] = row_ref[...]
    col_out[me_s] = col_ref[...]

    def wait_r(d, carry):
        row_copy(lax.rem(me_t + d, n_tgt), me_t).wait_send()
        j = lax.rem(me_t + n_tgt - d, n_tgt)
        row_copy(j, j).wait_recv()
        return carry
    lax.fori_loop(1, n_tgt, wait_r, 0)

    def wait_c(d, carry):
        col_copy(lax.rem(me_s + d, n_src), me_s).wait_send()
        j = lax.rem(me_s + n_src - d, n_src)
        col_copy(j, j).wait_recv()
        return carry
    lax.fori_loop(1, n_src, wait_c, 0)


def merge(gathered):
    tops, totals = gathered[:, 0], gathered[:, 1]
    best = jnp.max(tops, axis=0)
    return best, jnp.sum(totals * jnp.exp(tops - best[None]), axis=0)


def gather_stats(row_top, row_part, col_top, col_part):
    n_src = lax.axis_size("src")
    n_tgt = lax.axis_size("tgt")
    n_row, n_col = row_top.shape[0], col_top.shape[0]
    rows = jnp.stack([row_top, row_part]).reshape(2 * n_row // 128, 128)
    cols = jnp.stack([col_top, col_part]).reshape(2 * n_col // 128, 128)
    vmem = pl.BlockSpec(memory_space=pltpu.VMEM)
    row_all, col_all = pl.pallas_call(
        functools.partial(stats_gather_kernel, n_src, n_tgt),
        out_shape=(jax.ShapeDtypeStruct((n_tgt,) + rows.shape, jnp.float32),
                   jax.ShapeDtypeStruct((n_src,) + cols.shape, jnp.float32)),
        in_specs=[vmem, vmem],
        out_specs=(vmem, vmem),
        scratch_shapes=[
            pltpu.SemaphoreType.DMA((n_tgt,)),
            pltpu.SemaphoreType.DMA((n_tgt,)),
            pltpu.SemaphoreType.DMA((n_src,)),
            pltpu.SemaphoreType.DMA((n_src,)),
        ],
        compiler_params=pltpu.CompilerParams(collective_id=2, has_side_effects=True),
    )(rows, cols)
    row_top, row_total = merge(row_all.reshape(n_tgt, 2, n_row))
    col_top, col_total = merge(col_all.reshape(n_src, 2, n_col))
    return row_top, row_total, col_top, col_total


def body(source, target, start_map):
    highest = lax.Precision.HIGHEST
    score_scale = 2.0 / math.sqrt(source.shape[1])
    source_f32 = source.astype(jnp.float32)
    target_f32 = target.astype(jnp.float32)
    current = start_map
    for iteration in range(ITERS):
        mapped = jnp.dot(
            source, current.astype(jnp.bfloat16), preferred_element_type=jnp.float32
        ).astype(jnp.bfloat16)
        scores = (
            lax.dot_general(
                mapped, target, (((1,), (1,)), ((), ())), preferred_element_type=jnp.float32
            )
            * score_scale
        )
        row_local = jnp.max(scores, axis=1)
        col_local = jnp.max(scores, axis=0)
        row_part = jnp.sum(jnp.exp(scores - row_local[:, None]), axis=1)
        col_part = jnp.sum(jnp.exp(scores - col_local[None, :]), axis=0)
        row_top, row_total, col_top, col_total = gather_stats(row_local, row_part, col_local, col_part)
        row_weights = (jnp.exp(scores - row_top[:, None]) / row_total[:, None]).astype(jnp.bfloat16)
        col_weights = (jnp.exp(scores - col_top[None, :]) / col_total[None, :]).astype(jnp.bfloat16)
        source_part = jnp.dot(row_weights, target, preferred_element_type=jnp.float32)
        target_part = lax.dot_general(
            col_weights, source, (((0,), (0,)), ((), ())), preferred_element_type=jnp.float32
        )
        covariance = jnp.dot(source_f32.T, source_part, precision=highest)
        covariance = covariance + jnp.dot(target_part.T, target_f32, precision=highest)
        if iteration == ITERS - 1:
            source_soft = lax.psum_scatter(
                source_part, "tgt", scatter_dimension=0, tiled=True
            ).astype(jnp.bfloat16)
            covariance, target_soft = all_reduce(covariance, target_part)
        else:
            covariance = all_reduce(covariance)
        current = polar_steps(covariance)
    return (source_soft, target_soft, current)


def solution(mesh):
    in_specs = (P("src", None), P("tgt", None), P())
    out_specs = (P(("src", "tgt"), None), P("tgt", None), P())
    return jax.shard_map(body, mesh=mesh, in_specs=in_specs, out_specs=out_specs, check_vma=False)
```

```python
import math

import functools

import jax
import jax.numpy as jnp
from jax import lax
from jax.experimental import pallas as pl
from jax.experimental.pallas import tpu as pltpu
from jax.sharding import PartitionSpec as P

MESH = pl.DeviceIdType.MESH

ITERS = 2
NEWTON_STEPS = 8


def polar_steps(covariance):
    highest = lax.Precision.HIGH
    current = covariance / jnp.sqrt(jnp.sum(covariance * covariance) + 1e-06)

    def newton(step, current):
        gram_matrix = jnp.dot(current.T, current, precision=highest)
        return 1.5 * current - 0.5 * jnp.dot(current, gram_matrix, precision=highest)
    return lax.fori_loop(0, NEWTON_STEPS, newton, current)


def peer_barrier(n_src, n_tgt):
    me_s = lax.axis_index("src")
    me_t = lax.axis_index("tgt")
    barrier = pltpu.get_barrier_semaphore()

    def greet_src(d, carry):
        pl.semaphore_signal(barrier, 1, device_id=(lax.rem(me_s + d, n_src), me_t), device_id_type=MESH)
        return carry
    lax.fori_loop(1, n_src, greet_src, 0)

    def greet_tgt(d, carry):
        pl.semaphore_signal(barrier, 1, device_id=(me_s, lax.rem(me_t + d, n_tgt)), device_id_type=MESH)
        return carry
    lax.fori_loop(1, n_tgt, greet_tgt, 0)
    pl.semaphore_wait(barrier, n_src + n_tgt - 2)


def remote(src, dst, send, recv, device):
    return pltpu.make_async_remote_copy(
        src_ref=src, dst_ref=dst, send_sem=send, recv_sem=recv,
        device_id=device, device_id_type=MESH)


def start_all(me, n, device, src, slot, send, recv):
    def step(d, carry):
        k = lax.rem(me + d, n)
        remote(src(k), slot(me), send.at[k], recv.at[me], device(k)).start()
        return carry
    lax.fori_loop(1, n, step, 0)


def wait_all(me, n, device, src, slot, send, recv):
    def step(d, carry):
        k = lax.rem(me + d, n)
        remote(src(k), slot(me), send.at[k], recv.at[me], device(k)).wait_send()
        j = lax.rem(me + n - d, n)
        remote(src(j), slot(j), send.at[j], recv.at[j], device(j)).wait_recv()
        return carry
    lax.fori_loop(1, n, step, 0)


def all_reduce_kernel(n_src, n_tgt, with_target, *refs):
    if with_target:
        (xc, xt, oc, ot, gather_src, gather_tgt, g1, g2, s1,
         s_a, r_a, s_b, r_b, s_c, r_c, s_1, r_1, s_2, r_2, s_3, r_3, s_4, r_4) = refs
    else:
        xc, oc, gather_src, gather_tgt, s_a, r_a, s_b, r_b, s_c, r_c = refs
    me_s = lax.axis_index("src")
    me_t = lax.axis_index("tgt")
    peer_barrier(n_src, n_tgt)
    on_src = lambda k: (k, me_t)
    on_tgt = lambda k: (me_s, k)

    if with_target:
        n_y, n_z = xt.shape[0], xt.shape[1]
        my_z = me_s // n_y
        my_y = me_s % n_y
        on_y = lambda k: (my_z * n_y + k, me_t)
        on_z = lambda k: (k * n_y + my_y, me_t)
        start_all(my_y, n_y, on_y, lambda k: xt.at[k], lambda i: g1.at[i], s_1, r_1)
        g1[my_y] = xt[my_y]

    start_all(me_s, n_src, on_src, lambda k: xc.at[k], lambda i: gather_src.at[i], s_a, r_a)
    gather_src[me_s] = xc[me_s]
    wait_all(me_s, n_src, on_src, lambda k: xc.at[k], lambda i: gather_src.at[i], s_a, r_a)
    gather_tgt[me_t] = jnp.sum(gather_src[...], axis=0)

    if with_target:
        wait_all(my_y, n_y, on_y, lambda k: xt.at[k], lambda i: g1.at[i], s_1, r_1)
        s1[...] = jnp.sum(g1[...].astype(jnp.float32), axis=0).astype(s1.dtype)
        start_all(my_z, n_z, on_z, lambda k: s1.at[k], lambda i: g2.at[i], s_2, r_2)
        g2[my_z] = s1[my_z]

    start_all(me_t, n_tgt, on_tgt, lambda k: gather_tgt.at[me_t], lambda i: gather_tgt.at[i], s_b, r_b)
    wait_all(me_t, n_tgt, on_tgt, lambda k: gather_tgt.at[me_t], lambda i: gather_tgt.at[i], s_b, r_b)
    oc[me_s] = jnp.sum(gather_tgt[...], axis=0)
    start_all(me_s, n_src, on_src, lambda k: oc.at[me_s], lambda i: oc.at[i], s_c, r_c)

    if with_target:
        wait_all(my_z, n_z, on_z, lambda k: s1.at[k], lambda i: g2.at[i], s_2, r_2)
        ot[my_y, my_z] = jnp.sum(g2[...].astype(jnp.float32), axis=0).astype(ot.dtype)
        start_all(my_z, n_z, on_z, lambda k: ot.at[my_y, my_z], lambda i: ot.at[my_y, i], s_3, r_3)
    wait_all(me_s, n_src, on_src, lambda k: oc.at[me_s], lambda i: oc.at[i], s_c, r_c)
    if with_target:
        wait_all(my_z, n_z, on_z, lambda k: ot.at[my_y, my_z], lambda i: ot.at[my_y, i], s_3, r_3)
        start_all(my_y, n_y, on_y, lambda k: ot.at[my_y], lambda i: ot.at[i], s_4, r_4)
        wait_all(my_y, n_y, on_y, lambda k: ot.at[my_y], lambda i: ot.at[i], s_4, r_4)


def all_reduce(matrix, target_part=None):
    n_src = lax.axis_size("src")
    n_tgt = lax.axis_size("tgt")
    size = matrix.size
    lines = -(-size // 128)
    rows = -(-lines // (n_src * 8)) * 8
    flat = jnp.pad(matrix.reshape(-1), (0, n_src * rows * 128 - size)).reshape(n_src, rows, 128)
    vmem = pl.BlockSpec(memory_space=pltpu.VMEM)
    sems = [pltpu.SemaphoreType.DMA((n,)) for n in (n_src, n_src, n_tgt, n_tgt, n_src, n_src)]
    scratch = [pltpu.VMEM((n_src, rows, 128), jnp.float32), pltpu.VMEM((n_tgt, rows, 128), jnp.float32)]
    if target_part is None:
        out = pl.pallas_call(
            functools.partial(all_reduce_kernel, n_src, n_tgt, False),
            out_shape=jax.ShapeDtypeStruct(flat.shape, jnp.float32),
            in_specs=[vmem],
            out_specs=vmem,
            scratch_shapes=scratch + sems,
            compiler_params=pltpu.CompilerParams(collective_id=0, has_side_effects=True),
        )(flat)
        return out.reshape(-1)[:size].reshape(matrix.shape)
    t_rows, width = target_part.shape
    n_y = 4 if n_src % 4 == 0 else n_src
    n_z = n_src // n_y
    piece = t_rows // n_src
    chunks = target_part.astype(jnp.bfloat16).reshape(n_y, n_z, piece, width)
    out, target_sum = pl.pallas_call(
        functools.partial(all_reduce_kernel, n_src, n_tgt, True),
        out_shape=(jax.ShapeDtypeStruct(flat.shape, jnp.float32),
                   jax.ShapeDtypeStruct(chunks.shape, jnp.bfloat16)),
        in_specs=[vmem, vmem],
        out_specs=(vmem, vmem),
        scratch_shapes=scratch
        + [pltpu.VMEM(chunks.shape, jnp.bfloat16), pltpu.VMEM((n_z, piece, width), jnp.bfloat16),
           pltpu.VMEM((n_z, piece, width), jnp.bfloat16)]
        + sems
        + [pltpu.SemaphoreType.DMA((n,)) for n in (n_y, n_y, n_z, n_z, n_z, n_z, n_y, n_y)],
        compiler_params=pltpu.CompilerParams(collective_id=1, has_side_effects=True),
    )(flat, chunks)
    target_sum = target_sum.reshape(t_rows, width)
    return out.reshape(-1)[:size].reshape(matrix.shape), target_sum


def stats_gather_kernel(n_src, n_tgt, row_ref, col_ref, row_out, col_out,
                        send_r, recv_r, send_c, recv_c):
    me_s = lax.axis_index("src")
    me_t = lax.axis_index("tgt")
    peer_barrier(n_src, n_tgt)

    def row_copy(k, slot):
        return pltpu.make_async_remote_copy(
            src_ref=row_ref, dst_ref=row_out.at[slot], send_sem=send_r.at[k],
            recv_sem=recv_r.at[slot], device_id=(me_s, k), device_id_type=MESH)

    def col_copy(k, slot):
        return pltpu.make_async_remote_copy(
            src_ref=col_ref, dst_ref=col_out.at[slot], send_sem=send_c.at[k],
            recv_sem=recv_c.at[slot], device_id=(k, me_t), device_id_type=MESH)

    def start_c(d, carry):
        col_copy(lax.rem(me_s + d, n_src), me_s).start()
        return carry
    lax.fori_loop(1, n_src, start_c, 0)

    def start_r(d, carry):
        row_copy(lax.rem(me_t + d, n_tgt), me_t).start()
        return carry
    lax.fori_loop(1, n_tgt, start_r, 0)
    row_out[me_t] = row_ref[...]
    col_out[me_s] = col_ref[...]

    def wait_r(d, carry):
        row_copy(lax.rem(me_t + d, n_tgt), me_t).wait_send()
        j = lax.rem(me_t + n_tgt - d, n_tgt)
        row_copy(j, j).wait_recv()
        return carry
    lax.fori_loop(1, n_tgt, wait_r, 0)

    def wait_c(d, carry):
        col_copy(lax.rem(me_s + d, n_src), me_s).wait_send()
        j = lax.rem(me_s + n_src - d, n_src)
        col_copy(j, j).wait_recv()
        return carry
    lax.fori_loop(1, n_src, wait_c, 0)


def merge(gathered):
    tops, totals = gathered[:, 0], gathered[:, 1]
    best = jnp.max(tops, axis=0)
    return best, jnp.sum(totals * jnp.exp(tops - best[None]), axis=0)


def gather_stats(row_top, row_part, col_top, col_part):
    n_src = lax.axis_size("src")
    n_tgt = lax.axis_size("tgt")
    n_row, n_col = row_top.shape[0], col_top.shape[0]
    rows = jnp.stack([row_top, row_part]).reshape(2 * n_row // 128, 128)
    cols = jnp.stack([col_top, col_part]).reshape(2 * n_col // 128, 128)
    vmem = pl.BlockSpec(memory_space=pltpu.VMEM)
    row_all, col_all = pl.pallas_call(
        functools.partial(stats_gather_kernel, n_src, n_tgt),
        out_shape=(jax.ShapeDtypeStruct((n_tgt,) + rows.shape, jnp.float32),
                   jax.ShapeDtypeStruct((n_src,) + cols.shape, jnp.float32)),
        in_specs=[vmem, vmem],
        out_specs=(vmem, vmem),
        scratch_shapes=[
            pltpu.SemaphoreType.DMA((n_tgt,)),
            pltpu.SemaphoreType.DMA((n_tgt,)),
            pltpu.SemaphoreType.DMA((n_src,)),
            pltpu.SemaphoreType.DMA((n_src,)),
        ],
        compiler_params=pltpu.CompilerParams(collective_id=2, has_side_effects=True),
    )(rows, cols)
    row_top, row_total = merge(row_all.reshape(n_tgt, 2, n_row))
    col_top, col_total = merge(col_all.reshape(n_src, 2, n_col))
    return row_top, row_total, col_top, col_total


def body(source, target, start_map):
    highest = lax.Precision.HIGHEST
    score_scale = 2.0 / math.sqrt(source.shape[1])
    source_f32 = source.astype(jnp.float32)
    target_f32 = target.astype(jnp.float32)
    current = start_map
    for iteration in range(ITERS):
        mapped = jnp.dot(
            source, current.astype(jnp.bfloat16), preferred_element_type=jnp.float32
        ).astype(jnp.bfloat16)
        scores = (
            lax.dot_general(
                mapped, target, (((1,), (1,)), ((), ())), preferred_element_type=jnp.float32
            )
            * score_scale
        )
        row_local = jnp.max(scores, axis=1)
        col_local = jnp.max(scores, axis=0)
        row_part = jnp.sum(jnp.exp(scores - row_local[:, None]), axis=1)
        col_part = jnp.sum(jnp.exp(scores - col_local[None, :]), axis=0)
        row_top, row_total, col_top, col_total = gather_stats(row_local, row_part, col_local, col_part)
        row_weights = (jnp.exp(scores - row_top[:, None]) / row_total[:, None]).astype(jnp.bfloat16)
        col_weights = (jnp.exp(scores - col_top[None, :]) / col_total[None, :]).astype(jnp.bfloat16)
        source_part = jnp.dot(row_weights, target, preferred_element_type=jnp.float32)
        target_part = lax.dot_general(
            col_weights, source, (((0,), (0,)), ((), ())), preferred_element_type=jnp.float32
        )
        covariance = jnp.dot(source_f32.T, source_part, precision=highest)
        covariance = covariance + jnp.dot(target_part.T, target_f32, precision=highest)
        if iteration == ITERS - 1:
            source_soft = lax.psum_scatter(
                source_part, "tgt", scatter_dimension=0, tiled=True
            ).astype(jnp.bfloat16)
            covariance, target_soft = all_reduce(covariance, target_part)
        else:
            covariance = all_reduce(covariance)
        current = polar_steps(covariance)
    return (source_soft, target_soft, current)


def solution(mesh):
    in_specs = (P("src", None), P("tgt", None), P())
    out_specs = (P(("src", "tgt"), None), P("tgt", None), P())
    return jax.shard_map(body, mesh=mesh, in_specs=in_specs, out_specs=out_specs, check_vma=False)
```

```python
import math

import functools

import jax
import jax.numpy as jnp
from jax import lax
from jax.experimental import pallas as pl
from jax.experimental.pallas import tpu as pltpu
from jax.sharding import PartitionSpec as P

MESH = pl.DeviceIdType.MESH

ITERS = 2
NEWTON_STEPS = 8


def polar_steps(covariance):
    highest = lax.Precision.HIGH
    current = covariance / jnp.sqrt(jnp.sum(covariance * covariance) + 1e-06)

    def newton(step, current):
        gram_matrix = jnp.dot(current.T, current, precision=highest)
        return 1.5 * current - 0.5 * jnp.dot(current, gram_matrix, precision=highest)
    return lax.fori_loop(0, NEWTON_STEPS, newton, current)


def peer_barrier(n_src, n_tgt):
    me_s = lax.axis_index("src")
    me_t = lax.axis_index("tgt")
    barrier = pltpu.get_barrier_semaphore()

    def greet_src(d, carry):
        pl.semaphore_signal(barrier, 1, device_id=(lax.rem(me_s + d, n_src), me_t), device_id_type=MESH)
        return carry
    lax.fori_loop(1, n_src, greet_src, 0)

    def greet_tgt(d, carry):
        pl.semaphore_signal(barrier, 1, device_id=(me_s, lax.rem(me_t + d, n_tgt)), device_id_type=MESH)
        return carry
    lax.fori_loop(1, n_tgt, greet_tgt, 0)
    pl.semaphore_wait(barrier, n_src + n_tgt - 2)


def remote(src, dst, send, recv, device):
    return pltpu.make_async_remote_copy(
        src_ref=src, dst_ref=dst, send_sem=send, recv_sem=recv,
        device_id=device, device_id_type=MESH)


def start_all(me, n, device, src, slot, send, recv):
    def step(d, carry):
        k = lax.rem(me + d, n)
        remote(src(k), slot(me), send.at[k], recv.at[me], device(k)).start()
        return carry
    lax.fori_loop(1, n, step, 0)


def wait_all(me, n, device, src, slot, send, recv):
    def step(d, carry):
        k = lax.rem(me + d, n)
        remote(src(k), slot(me), send.at[k], recv.at[me], device(k)).wait_send()
        j = lax.rem(me + n - d, n)
        remote(src(j), slot(j), send.at[j], recv.at[j], device(j)).wait_recv()
        return carry
    lax.fori_loop(1, n, step, 0)


def all_reduce_kernel(n_src, n_tgt, with_target, *refs):
    if with_target:
        (xc, xt, xs, oc, ot, os, gather_src, gather_tgt, g1, g2, s1, gs,
         s_a, r_a, s_b, r_b, s_c, r_c, s_1, r_1, s_2, r_2, s_3, r_3, s_4, r_4, s_s, r_s) = refs
    else:
        xc, oc, gather_src, gather_tgt, s_a, r_a, s_b, r_b, s_c, r_c = refs
    me_s = lax.axis_index("src")
    me_t = lax.axis_index("tgt")
    peer_barrier(n_src, n_tgt)
    on_src = lambda k: (k, me_t)
    on_tgt = lambda k: (me_s, k)

    if with_target:
        n_y, n_z = xt.shape[0], xt.shape[1]
        my_z = me_s // n_y
        my_y = me_s % n_y
        on_y = lambda k: (my_z * n_y + k, me_t)
        on_z = lambda k: (k * n_y + my_y, me_t)
        start_all(my_y, n_y, on_y, lambda k: xt.at[k], lambda i: g1.at[i], s_1, r_1)
        start_all(me_t, n_tgt, on_tgt, lambda k: xs.at[k], lambda i: gs.at[i], s_s, r_s)
        g1[my_y] = xt[my_y]
        gs[me_t] = xs[me_t]

    start_all(me_s, n_src, on_src, lambda k: xc.at[k], lambda i: gather_src.at[i], s_a, r_a)
    gather_src[me_s] = xc[me_s]
    wait_all(me_s, n_src, on_src, lambda k: xc.at[k], lambda i: gather_src.at[i], s_a, r_a)
    gather_tgt[me_t] = jnp.sum(gather_src[...], axis=0)

    if with_target:
        wait_all(my_y, n_y, on_y, lambda k: xt.at[k], lambda i: g1.at[i], s_1, r_1)
        s1[...] = jnp.sum(g1[...].astype(jnp.float32), axis=0).astype(s1.dtype)
        start_all(my_z, n_z, on_z, lambda k: s1.at[k], lambda i: g2.at[i], s_2, r_2)
        g2[my_z] = s1[my_z]

    start_all(me_t, n_tgt, on_tgt, lambda k: gather_tgt.at[me_t], lambda i: gather_tgt.at[i], s_b, r_b)
    wait_all(me_t, n_tgt, on_tgt, lambda k: gather_tgt.at[me_t], lambda i: gather_tgt.at[i], s_b, r_b)
    oc[me_s] = jnp.sum(gather_tgt[...], axis=0)
    start_all(me_s, n_src, on_src, lambda k: oc.at[me_s], lambda i: oc.at[i], s_c, r_c)

    if with_target:
        wait_all(my_z, n_z, on_z, lambda k: s1.at[k], lambda i: g2.at[i], s_2, r_2)
        ot[my_y, my_z] = jnp.sum(g2[...].astype(jnp.float32), axis=0).astype(ot.dtype)
        start_all(my_z, n_z, on_z, lambda k: ot.at[my_y, my_z], lambda i: ot.at[my_y, i], s_3, r_3)
    wait_all(me_s, n_src, on_src, lambda k: oc.at[me_s], lambda i: oc.at[i], s_c, r_c)
    if with_target:
        wait_all(my_z, n_z, on_z, lambda k: ot.at[my_y, my_z], lambda i: ot.at[my_y, i], s_3, r_3)
        start_all(my_y, n_y, on_y, lambda k: ot.at[my_y], lambda i: ot.at[i], s_4, r_4)
        wait_all(me_t, n_tgt, on_tgt, lambda k: xs.at[k], lambda i: gs.at[i], s_s, r_s)
        os[...] = jnp.sum(gs[...], axis=0).astype(os.dtype)
        wait_all(my_y, n_y, on_y, lambda k: ot.at[my_y], lambda i: ot.at[i], s_4, r_4)


def all_reduce(matrix, target_part=None, source_part=None):
    n_src = lax.axis_size("src")
    n_tgt = lax.axis_size("tgt")
    size = matrix.size
    lines = -(-size // 128)
    rows = -(-lines // (n_src * 8)) * 8
    flat = jnp.pad(matrix.reshape(-1), (0, n_src * rows * 128 - size)).reshape(n_src, rows, 128)
    vmem = pl.BlockSpec(memory_space=pltpu.VMEM)
    sems = [pltpu.SemaphoreType.DMA((n,)) for n in (n_src, n_src, n_tgt, n_tgt, n_src, n_src)]
    scratch = [pltpu.VMEM((n_src, rows, 128), jnp.float32), pltpu.VMEM((n_tgt, rows, 128), jnp.float32)]
    if target_part is None:
        out = pl.pallas_call(
            functools.partial(all_reduce_kernel, n_src, n_tgt, False),
            out_shape=jax.ShapeDtypeStruct(flat.shape, jnp.float32),
            in_specs=[vmem],
            out_specs=vmem,
            scratch_shapes=scratch + sems,
            compiler_params=pltpu.CompilerParams(collective_id=0, has_side_effects=True),
        )(flat)
        return out.reshape(-1)[:size].reshape(matrix.shape)
    t_rows, width = target_part.shape
    n_y = 4 if n_src % 4 == 0 else n_src
    n_z = n_src // n_y
    piece = t_rows // n_src
    chunks = target_part.astype(jnp.bfloat16).reshape(n_y, n_z, piece, width)
    s_rows = source_part.shape[0]
    pieces = source_part.reshape(n_tgt, s_rows // n_tgt, width)
    out, target_sum, source_sum = pl.pallas_call(
        functools.partial(all_reduce_kernel, n_src, n_tgt, True),
        out_shape=(jax.ShapeDtypeStruct(flat.shape, jnp.float32),
                   jax.ShapeDtypeStruct(chunks.shape, jnp.bfloat16),
                   jax.ShapeDtypeStruct(pieces.shape[1:], jnp.bfloat16)),
        in_specs=[vmem, vmem, vmem],
        out_specs=(vmem, vmem, vmem),
        scratch_shapes=scratch
        + [pltpu.VMEM(chunks.shape, jnp.bfloat16), pltpu.VMEM((n_z, piece, width), jnp.bfloat16),
           pltpu.VMEM((n_z, piece, width), jnp.bfloat16), pltpu.VMEM(pieces.shape, jnp.float32)]
        + sems
        + [pltpu.SemaphoreType.DMA((n,)) for n in (n_y, n_y, n_z, n_z, n_z, n_z, n_y, n_y, n_tgt, n_tgt)],
        compiler_params=pltpu.CompilerParams(collective_id=1, has_side_effects=True),
    )(flat, chunks, pieces)
    target_sum = target_sum.reshape(t_rows, width)
    return out.reshape(-1)[:size].reshape(matrix.shape), target_sum, source_sum


def stats_gather_kernel(n_src, n_tgt, row_ref, col_ref, row_out, col_out,
                        send_r, recv_r, send_c, recv_c):
    me_s = lax.axis_index("src")
    me_t = lax.axis_index("tgt")
    peer_barrier(n_src, n_tgt)

    def row_copy(k, slot):
        return pltpu.make_async_remote_copy(
            src_ref=row_ref, dst_ref=row_out.at[slot], send_sem=send_r.at[k],
            recv_sem=recv_r.at[slot], device_id=(me_s, k), device_id_type=MESH)

    def col_copy(k, slot):
        return pltpu.make_async_remote_copy(
            src_ref=col_ref, dst_ref=col_out.at[slot], send_sem=send_c.at[k],
            recv_sem=recv_c.at[slot], device_id=(k, me_t), device_id_type=MESH)

    def start_c(d, carry):
        col_copy(lax.rem(me_s + d, n_src), me_s).start()
        return carry
    lax.fori_loop(1, n_src, start_c, 0)

    def start_r(d, carry):
        row_copy(lax.rem(me_t + d, n_tgt), me_t).start()
        return carry
    lax.fori_loop(1, n_tgt, start_r, 0)
    row_out[me_t] = row_ref[...]
    col_out[me_s] = col_ref[...]

    def wait_r(d, carry):
        row_copy(lax.rem(me_t + d, n_tgt), me_t).wait_send()
        j = lax.rem(me_t + n_tgt - d, n_tgt)
        row_copy(j, j).wait_recv()
        return carry
    lax.fori_loop(1, n_tgt, wait_r, 0)

    def wait_c(d, carry):
        col_copy(lax.rem(me_s + d, n_src), me_s).wait_send()
        j = lax.rem(me_s + n_src - d, n_src)
        col_copy(j, j).wait_recv()
        return carry
    lax.fori_loop(1, n_src, wait_c, 0)


def merge(gathered):
    tops, totals = gathered[:, 0], gathered[:, 1]
    best = jnp.max(tops, axis=0)
    return best, jnp.sum(totals * jnp.exp(tops - best[None]), axis=0)


def gather_stats(row_top, row_part, col_top, col_part):
    n_src = lax.axis_size("src")
    n_tgt = lax.axis_size("tgt")
    n_row, n_col = row_top.shape[0], col_top.shape[0]
    rows = jnp.stack([row_top, row_part]).reshape(2 * n_row // 128, 128)
    cols = jnp.stack([col_top, col_part]).reshape(2 * n_col // 128, 128)
    vmem = pl.BlockSpec(memory_space=pltpu.VMEM)
    row_all, col_all = pl.pallas_call(
        functools.partial(stats_gather_kernel, n_src, n_tgt),
        out_shape=(jax.ShapeDtypeStruct((n_tgt,) + rows.shape, jnp.float32),
                   jax.ShapeDtypeStruct((n_src,) + cols.shape, jnp.float32)),
        in_specs=[vmem, vmem],
        out_specs=(vmem, vmem),
        scratch_shapes=[
            pltpu.SemaphoreType.DMA((n_tgt,)),
            pltpu.SemaphoreType.DMA((n_tgt,)),
            pltpu.SemaphoreType.DMA((n_src,)),
            pltpu.SemaphoreType.DMA((n_src,)),
        ],
        compiler_params=pltpu.CompilerParams(collective_id=2, has_side_effects=True),
    )(rows, cols)
    row_top, row_total = merge(row_all.reshape(n_tgt, 2, n_row))
    col_top, col_total = merge(col_all.reshape(n_src, 2, n_col))
    return row_top, row_total, col_top, col_total


def body(source, target, start_map):
    highest = lax.Precision.HIGHEST
    score_scale = 2.0 / math.sqrt(source.shape[1])
    source_f32 = source.astype(jnp.float32)
    target_f32 = target.astype(jnp.float32)
    current = start_map
    for iteration in range(ITERS):
        mapped = jnp.dot(
            source, current.astype(jnp.bfloat16), preferred_element_type=jnp.float32
        ).astype(jnp.bfloat16)
        scores = (
            lax.dot_general(
                mapped, target, (((1,), (1,)), ((), ())), preferred_element_type=jnp.float32
            )
            * score_scale
        )
        row_local = jnp.max(scores, axis=1)
        col_local = jnp.max(scores, axis=0)
        row_part = jnp.sum(jnp.exp(scores - row_local[:, None]), axis=1)
        col_part = jnp.sum(jnp.exp(scores - col_local[None, :]), axis=0)
        row_top, row_total, col_top, col_total = gather_stats(row_local, row_part, col_local, col_part)
        row_weights = (jnp.exp(scores - row_top[:, None]) / row_total[:, None]).astype(jnp.bfloat16)
        col_weights = (jnp.exp(scores - col_top[None, :]) / col_total[None, :]).astype(jnp.bfloat16)
        source_part = jnp.dot(row_weights, target, preferred_element_type=jnp.float32)
        target_part = lax.dot_general(
            col_weights, source, (((0,), (0,)), ((), ())), preferred_element_type=jnp.float32
        )
        covariance = jnp.dot(source_f32.T, source_part, precision=highest)
        covariance = covariance + jnp.dot(target_part.T, target_f32, precision=highest)
        if iteration == ITERS - 1:
            covariance, target_soft, source_soft = all_reduce(covariance, target_part, source_part)
        else:
            covariance = all_reduce(covariance)
        current = polar_steps(covariance)
    return (source_soft, target_soft, current)


def solution(mesh):
    in_specs = (P("src", None), P("tgt", None), P())
    out_specs = (P(("src", "tgt"), None), P("tgt", None), P())
    return jax.shard_map(body, mesh=mesh, in_specs=in_specs, out_specs=out_specs, check_vma=False)
```

```python
import math

import functools

import jax
import jax.numpy as jnp
from jax import lax
from jax.experimental import pallas as pl
from jax.experimental.pallas import tpu as pltpu
from jax.sharding import PartitionSpec as P

MESH = pl.DeviceIdType.MESH

ITERS = 2
NEWTON_STEPS = 8


def polar_kernel(steps, c_ref, o_ref):
    highest = lax.Precision.HIGHEST
    c = c_ref[...]
    norm = jnp.sum(jnp.sum(c * c, axis=1, keepdims=True), axis=0, keepdims=True)
    current = c / jnp.sqrt(norm + 1e-06)

    def newton(step, current):
        outer = lax.dot_general(current, current, (((1,), (1,)), ((), ())),
                                precision=highest, preferred_element_type=jnp.float32)
        return 1.5 * current - 0.5 * jnp.dot(outer, current, precision=highest,
                                              preferred_element_type=jnp.float32)
    o_ref[...] = lax.fori_loop(0, steps, newton, current)


def polar_steps(covariance):
    size = covariance.shape[0]
    padded = -(-size // 128) * 128
    c = jnp.pad(covariance, ((0, padded - size), (0, padded - size)))
    vmem = pl.BlockSpec(memory_space=pltpu.VMEM)
    out = pl.pallas_call(
        functools.partial(polar_kernel, NEWTON_STEPS),
        out_shape=jax.ShapeDtypeStruct(c.shape, jnp.float32),
        in_specs=[vmem],
        out_specs=vmem,
    )(c)
    return out[:size, :size]


def peer_barrier(n_src, n_tgt):
    me_s = lax.axis_index("src")
    me_t = lax.axis_index("tgt")
    barrier = pltpu.get_barrier_semaphore()

    def greet_src(d, carry):
        pl.semaphore_signal(barrier, 1, device_id=(lax.rem(me_s + d, n_src), me_t), device_id_type=MESH)
        return carry
    lax.fori_loop(1, n_src, greet_src, 0)

    def greet_tgt(d, carry):
        pl.semaphore_signal(barrier, 1, device_id=(me_s, lax.rem(me_t + d, n_tgt)), device_id_type=MESH)
        return carry
    lax.fori_loop(1, n_tgt, greet_tgt, 0)
    pl.semaphore_wait(barrier, n_src + n_tgt - 2)


def remote(src, dst, send, recv, device):
    return pltpu.make_async_remote_copy(
        src_ref=src, dst_ref=dst, send_sem=send, recv_sem=recv,
        device_id=device, device_id_type=MESH)


def start_all(me, n, device, src, slot, send, recv):
    def step(d, carry):
        k = lax.rem(me + d, n)
        remote(src(k), slot(me), send.at[k], recv.at[me], device(k)).start()
        return carry
    lax.fori_loop(1, n, step, 0)


def wait_all(me, n, device, src, slot, send, recv):
    def step(d, carry):
        k = lax.rem(me + d, n)
        remote(src(k), slot(me), send.at[k], recv.at[me], device(k)).wait_send()
        j = lax.rem(me + n - d, n)
        remote(src(j), slot(j), send.at[j], recv.at[j], device(j)).wait_recv()
        return carry
    lax.fori_loop(1, n, step, 0)


def all_reduce_kernel(n_src, n_tgt, with_target, *refs):
    if with_target:
        (xc, xt, xs, oc, ot, os, gather_src, gather_tgt, g1, g2, s1, gs,
         s_a, r_a, s_b, r_b, s_c, r_c, s_1, r_1, s_2, r_2, s_3, r_3, s_4, r_4, s_s, r_s) = refs
    else:
        xc, oc, gather_src, gather_tgt, s_a, r_a, s_b, r_b, s_c, r_c = refs
    me_s = lax.axis_index("src")
    me_t = lax.axis_index("tgt")
    peer_barrier(n_src, n_tgt)
    on_src = lambda k: (k, me_t)
    on_tgt = lambda k: (me_s, k)

    if with_target:
        n_y, n_z = xt.shape[0], xt.shape[1]
        my_z = me_s // n_y
        my_y = me_s % n_y
        on_y = lambda k: (my_z * n_y + k, me_t)
        on_z = lambda k: (k * n_y + my_y, me_t)
        start_all(my_y, n_y, on_y, lambda k: xt.at[k], lambda i: g1.at[i], s_1, r_1)
        start_all(me_t, n_tgt, on_tgt, lambda k: xs.at[k], lambda i: gs.at[i], s_s, r_s)
        g1[my_y] = xt[my_y]
        gs[me_t] = xs[me_t]

    start_all(me_s, n_src, on_src, lambda k: xc.at[k], lambda i: gather_src.at[i], s_a, r_a)
    gather_src[me_s] = xc[me_s]
    wait_all(me_s, n_src, on_src, lambda k: xc.at[k], lambda i: gather_src.at[i], s_a, r_a)
    gather_tgt[me_t] = jnp.sum(gather_src[...], axis=0)

    if with_target:
        wait_all(my_y, n_y, on_y, lambda k: xt.at[k], lambda i: g1.at[i], s_1, r_1)
        s1[...] = jnp.sum(g1[...].astype(jnp.float32), axis=0).astype(s1.dtype)
        start_all(my_z, n_z, on_z, lambda k: s1.at[k], lambda i: g2.at[i], s_2, r_2)
        g2[my_z] = s1[my_z]

    start_all(me_t, n_tgt, on_tgt, lambda k: gather_tgt.at[me_t], lambda i: gather_tgt.at[i], s_b, r_b)
    wait_all(me_t, n_tgt, on_tgt, lambda k: gather_tgt.at[me_t], lambda i: gather_tgt.at[i], s_b, r_b)
    oc[me_s] = jnp.sum(gather_tgt[...], axis=0)
    start_all(me_s, n_src, on_src, lambda k: oc.at[me_s], lambda i: oc.at[i], s_c, r_c)

    if with_target:
        wait_all(my_z, n_z, on_z, lambda k: s1.at[k], lambda i: g2.at[i], s_2, r_2)
        ot[my_y, my_z] = jnp.sum(g2[...].astype(jnp.float32), axis=0).astype(ot.dtype)
        start_all(my_z, n_z, on_z, lambda k: ot.at[my_y, my_z], lambda i: ot.at[my_y, i], s_3, r_3)
    wait_all(me_s, n_src, on_src, lambda k: oc.at[me_s], lambda i: oc.at[i], s_c, r_c)
    if with_target:
        wait_all(my_z, n_z, on_z, lambda k: ot.at[my_y, my_z], lambda i: ot.at[my_y, i], s_3, r_3)
        start_all(my_y, n_y, on_y, lambda k: ot.at[my_y], lambda i: ot.at[i], s_4, r_4)
        wait_all(me_t, n_tgt, on_tgt, lambda k: xs.at[k], lambda i: gs.at[i], s_s, r_s)
        os[...] = jnp.sum(gs[...], axis=0).astype(os.dtype)
        wait_all(my_y, n_y, on_y, lambda k: ot.at[my_y], lambda i: ot.at[i], s_4, r_4)


def all_reduce(matrix, target_part=None, source_part=None):
    n_src = lax.axis_size("src")
    n_tgt = lax.axis_size("tgt")
    size = matrix.size
    lines = -(-size // 128)
    rows = -(-lines // (n_src * 8)) * 8
    flat = jnp.pad(matrix.reshape(-1), (0, n_src * rows * 128 - size)).reshape(n_src, rows, 128)
    vmem = pl.BlockSpec(memory_space=pltpu.VMEM)
    sems = [pltpu.SemaphoreType.DMA((n,)) for n in (n_src, n_src, n_tgt, n_tgt, n_src, n_src)]
    scratch = [pltpu.VMEM((n_src, rows, 128), jnp.float32), pltpu.VMEM((n_tgt, rows, 128), jnp.float32)]
    if target_part is None:
        out = pl.pallas_call(
            functools.partial(all_reduce_kernel, n_src, n_tgt, False),
            out_shape=jax.ShapeDtypeStruct(flat.shape, jnp.float32),
            in_specs=[vmem],
            out_specs=vmem,
            scratch_shapes=scratch + sems,
            compiler_params=pltpu.CompilerParams(collective_id=0, has_side_effects=True),
        )(flat)
        return out.reshape(-1)[:size].reshape(matrix.shape)
    t_rows, width = target_part.shape
    n_y = 4 if n_src % 4 == 0 else n_src
    n_z = n_src // n_y
    piece = t_rows // n_src
    chunks = target_part.astype(jnp.bfloat16).reshape(n_y, n_z, piece, width)
    s_rows = source_part.shape[0]
    pieces = source_part.reshape(n_tgt, s_rows // n_tgt, width)
    out, target_sum, source_sum = pl.pallas_call(
        functools.partial(all_reduce_kernel, n_src, n_tgt, True),
        out_shape=(jax.ShapeDtypeStruct(flat.shape, jnp.float32),
                   jax.ShapeDtypeStruct(chunks.shape, jnp.bfloat16),
                   jax.ShapeDtypeStruct(pieces.shape[1:], jnp.bfloat16)),
        in_specs=[vmem, vmem, vmem],
        out_specs=(vmem, vmem, vmem),
        scratch_shapes=scratch
        + [pltpu.VMEM(chunks.shape, jnp.bfloat16), pltpu.VMEM((n_z, piece, width), jnp.bfloat16),
           pltpu.VMEM((n_z, piece, width), jnp.bfloat16), pltpu.VMEM(pieces.shape, jnp.float32)]
        + sems
        + [pltpu.SemaphoreType.DMA((n,)) for n in (n_y, n_y, n_z, n_z, n_z, n_z, n_y, n_y, n_tgt, n_tgt)],
        compiler_params=pltpu.CompilerParams(collective_id=1, has_side_effects=True),
    )(flat, chunks, pieces)
    target_sum = target_sum.reshape(t_rows, width)
    return out.reshape(-1)[:size].reshape(matrix.shape), target_sum, source_sum


def stats_gather_kernel(n_src, n_tgt, row_ref, col_ref, row_out, col_out,
                        send_r, recv_r, send_c, recv_c):
    me_s = lax.axis_index("src")
    me_t = lax.axis_index("tgt")
    peer_barrier(n_src, n_tgt)

    def row_copy(k, slot):
        return pltpu.make_async_remote_copy(
            src_ref=row_ref, dst_ref=row_out.at[slot], send_sem=send_r.at[k],
            recv_sem=recv_r.at[slot], device_id=(me_s, k), device_id_type=MESH)

    def col_copy(k, slot):
        return pltpu.make_async_remote_copy(
            src_ref=col_ref, dst_ref=col_out.at[slot], send_sem=send_c.at[k],
            recv_sem=recv_c.at[slot], device_id=(k, me_t), device_id_type=MESH)

    def start_c(d, carry):
        col_copy(lax.rem(me_s + d, n_src), me_s).start()
        return carry
    lax.fori_loop(1, n_src, start_c, 0)

    def start_r(d, carry):
        row_copy(lax.rem(me_t + d, n_tgt), me_t).start()
        return carry
    lax.fori_loop(1, n_tgt, start_r, 0)
    row_out[me_t] = row_ref[...]
    col_out[me_s] = col_ref[...]

    def wait_r(d, carry):
        row_copy(lax.rem(me_t + d, n_tgt), me_t).wait_send()
        j = lax.rem(me_t + n_tgt - d, n_tgt)
        row_copy(j, j).wait_recv()
        return carry
    lax.fori_loop(1, n_tgt, wait_r, 0)

    def wait_c(d, carry):
        col_copy(lax.rem(me_s + d, n_src), me_s).wait_send()
        j = lax.rem(me_s + n_src - d, n_src)
        col_copy(j, j).wait_recv()
        return carry
    lax.fori_loop(1, n_src, wait_c, 0)


def merge(gathered):
    tops, totals = gathered[:, 0], gathered[:, 1]
    best = jnp.max(tops, axis=0)
    return best, jnp.sum(totals * jnp.exp(tops - best[None]), axis=0)


def gather_stats(row_top, row_part, col_top, col_part):
    n_src = lax.axis_size("src")
    n_tgt = lax.axis_size("tgt")
    n_row, n_col = row_top.shape[0], col_top.shape[0]
    rows = jnp.stack([row_top, row_part]).reshape(2 * n_row // 128, 128)
    cols = jnp.stack([col_top, col_part]).reshape(2 * n_col // 128, 128)
    vmem = pl.BlockSpec(memory_space=pltpu.VMEM)
    row_all, col_all = pl.pallas_call(
        functools.partial(stats_gather_kernel, n_src, n_tgt),
        out_shape=(jax.ShapeDtypeStruct((n_tgt,) + rows.shape, jnp.float32),
                   jax.ShapeDtypeStruct((n_src,) + cols.shape, jnp.float32)),
        in_specs=[vmem, vmem],
        out_specs=(vmem, vmem),
        scratch_shapes=[
            pltpu.SemaphoreType.DMA((n_tgt,)),
            pltpu.SemaphoreType.DMA((n_tgt,)),
            pltpu.SemaphoreType.DMA((n_src,)),
            pltpu.SemaphoreType.DMA((n_src,)),
        ],
        compiler_params=pltpu.CompilerParams(collective_id=2, has_side_effects=True),
    )(rows, cols)
    row_top, row_total = merge(row_all.reshape(n_tgt, 2, n_row))
    col_top, col_total = merge(col_all.reshape(n_src, 2, n_col))
    return row_top, row_total, col_top, col_total


def body(source, target, start_map):
    highest = lax.Precision.HIGHEST
    score_scale = 2.0 / math.sqrt(source.shape[1])
    source_f32 = source.astype(jnp.float32)
    target_f32 = target.astype(jnp.float32)
    current = start_map
    for iteration in range(ITERS):
        mapped = jnp.dot(
            source, current.astype(jnp.bfloat16), preferred_element_type=jnp.float32
        ).astype(jnp.bfloat16)
        scores = (
            lax.dot_general(
                mapped, target, (((1,), (1,)), ((), ())), preferred_element_type=jnp.float32
            )
            * score_scale
        )
        row_local = jnp.max(scores, axis=1)
        col_local = jnp.max(scores, axis=0)
        row_part = jnp.sum(jnp.exp(scores - row_local[:, None]), axis=1)
        col_part = jnp.sum(jnp.exp(scores - col_local[None, :]), axis=0)
        row_top, row_total, col_top, col_total = gather_stats(row_local, row_part, col_local, col_part)
        row_weights = (jnp.exp(scores - row_top[:, None]) / row_total[:, None]).astype(jnp.bfloat16)
        col_weights = (jnp.exp(scores - col_top[None, :]) / col_total[None, :]).astype(jnp.bfloat16)
        source_part = jnp.dot(row_weights, target, preferred_element_type=jnp.float32)
        target_part = lax.dot_general(
            col_weights, source, (((0,), (0,)), ((), ())), preferred_element_type=jnp.float32
        )
        covariance = jnp.dot(source_f32.T, source_part, precision=highest)
        covariance = covariance + jnp.dot(target_part.T, target_f32, precision=highest)
        if iteration == ITERS - 1:
            covariance, target_soft, source_soft = all_reduce(covariance, target_part, source_part)
        else:
            covariance = all_reduce(covariance)
        current = polar_steps(covariance)
    return (source_soft, target_soft, current)


def solution(mesh):
    in_specs = (P("src", None), P("tgt", None), P())
    out_specs = (P(("src", "tgt"), None), P("tgt", None), P())
    return jax.shard_map(body, mesh=mesh, in_specs=in_specs, out_specs=out_specs, check_vma=False)
```

```python
import math

import functools

import jax
import jax.numpy as jnp
from jax import lax
from jax.experimental import pallas as pl
from jax.experimental.pallas import tpu as pltpu
from jax.sharding import PartitionSpec as P

MESH = pl.DeviceIdType.MESH

ITERS = 2
NEWTON_STEPS = 8


def polar_steps(covariance):
    highest = lax.Precision.HIGH
    current = covariance / jnp.sqrt(jnp.sum(covariance * covariance) + 1e-06)

    def newton(step, current):
        gram_matrix = jnp.dot(current.T, current, precision=highest)
        return 1.5 * current - 0.5 * jnp.dot(current, gram_matrix, precision=highest)
    return lax.fori_loop(0, NEWTON_STEPS, newton, current)


def peer_barrier(n_src, n_tgt):
    me_s = lax.axis_index("src")
    me_t = lax.axis_index("tgt")
    barrier = pltpu.get_barrier_semaphore()

    def greet_src(d, carry):
        pl.semaphore_signal(barrier, 1, device_id=(lax.rem(me_s + d, n_src), me_t), device_id_type=MESH)
        return carry
    lax.fori_loop(1, n_src, greet_src, 0)

    def greet_tgt(d, carry):
        pl.semaphore_signal(barrier, 1, device_id=(me_s, lax.rem(me_t + d, n_tgt)), device_id_type=MESH)
        return carry
    lax.fori_loop(1, n_tgt, greet_tgt, 0)
    pl.semaphore_wait(barrier, n_src + n_tgt - 2)


def remote(src, dst, send, recv, device):
    return pltpu.make_async_remote_copy(
        src_ref=src, dst_ref=dst, send_sem=send, recv_sem=recv,
        device_id=device, device_id_type=MESH)


def start_all(me, n, device, src, slot, send, recv):
    def step(d, carry):
        k = lax.rem(me + d, n)
        remote(src(k), slot(me), send.at[k], recv.at[me], device(k)).start()
        return carry
    lax.fori_loop(1, n, step, 0)


def wait_all(me, n, device, src, slot, send, recv):
    def step(d, carry):
        k = lax.rem(me + d, n)
        remote(src(k), slot(me), send.at[k], recv.at[me], device(k)).wait_send()
        j = lax.rem(me + n - d, n)
        remote(src(j), slot(j), send.at[j], recv.at[j], device(j)).wait_recv()
        return carry
    lax.fori_loop(1, n, step, 0)


def all_reduce_kernel(n_src, n_tgt, with_target, *refs):
    if with_target:
        (xc, xt, xs, oc, ot, os, gather_src, gather_tgt, g1, g2, s1, gs,
         s_a, r_a, s_b, r_b, s_c, r_c, s_1, r_1, s_2, r_2, s_3, r_3, s_4, r_4, s_s, r_s) = refs
    else:
        xc, oc, gather_src, gather_tgt, s_a, r_a, s_b, r_b, s_c, r_c = refs
    me_s = lax.axis_index("src")
    me_t = lax.axis_index("tgt")
    peer_barrier(n_src, n_tgt)
    on_src = lambda k: (k, me_t)
    on_tgt = lambda k: (me_s, k)

    if with_target:
        n_y, n_z = xt.shape[0], xt.shape[1]
        my_z = me_s // n_y
        my_y = me_s % n_y
        on_y = lambda k: (my_z * n_y + k, me_t)
        on_z = lambda k: (k * n_y + my_y, me_t)
        start_all(my_y, n_y, on_y, lambda k: xt.at[k], lambda i: g1.at[i], s_1, r_1)
        start_all(me_t, n_tgt, on_tgt, lambda k: xs.at[k], lambda i: gs.at[i], s_s, r_s)
        g1[my_y] = xt[my_y]
        gs[me_t] = xs[me_t]

    start_all(me_s, n_src, on_src, lambda k: xc.at[k], lambda i: gather_src.at[i], s_a, r_a)
    gather_src[me_s] = xc[me_s]
    wait_all(me_s, n_src, on_src, lambda k: xc.at[k], lambda i: gather_src.at[i], s_a, r_a)
    gather_tgt[me_t] = jnp.sum(gather_src[...], axis=0)

    if with_target:
        wait_all(my_y, n_y, on_y, lambda k: xt.at[k], lambda i: g1.at[i], s_1, r_1)
        s1[...] = jnp.sum(g1[...].astype(jnp.float32), axis=0).astype(s1.dtype)
        start_all(my_z, n_z, on_z, lambda k: s1.at[k], lambda i: g2.at[i], s_2, r_2)
        g2[my_z] = s1[my_z]

    start_all(me_t, n_tgt, on_tgt, lambda k: gather_tgt.at[me_t], lambda i: gather_tgt.at[i], s_b, r_b)
    wait_all(me_t, n_tgt, on_tgt, lambda k: gather_tgt.at[me_t], lambda i: gather_tgt.at[i], s_b, r_b)
    oc[me_s] = jnp.sum(gather_tgt[...], axis=0)
    start_all(me_s, n_src, on_src, lambda k: oc.at[me_s], lambda i: oc.at[i], s_c, r_c)

    if with_target:
        wait_all(my_z, n_z, on_z, lambda k: s1.at[k], lambda i: g2.at[i], s_2, r_2)
        ot[my_y, my_z] = jnp.sum(g2[...].astype(jnp.float32), axis=0).astype(ot.dtype)
        start_all(my_z, n_z, on_z, lambda k: ot.at[my_y, my_z], lambda i: ot.at[my_y, i], s_3, r_3)
    wait_all(me_s, n_src, on_src, lambda k: oc.at[me_s], lambda i: oc.at[i], s_c, r_c)
    if with_target:
        wait_all(my_z, n_z, on_z, lambda k: ot.at[my_y, my_z], lambda i: ot.at[my_y, i], s_3, r_3)
        start_all(my_y, n_y, on_y, lambda k: ot.at[my_y], lambda i: ot.at[i], s_4, r_4)
        wait_all(me_t, n_tgt, on_tgt, lambda k: xs.at[k], lambda i: gs.at[i], s_s, r_s)
        os[...] = jnp.sum(gs[...].astype(jnp.float32), axis=0).astype(os.dtype)
        wait_all(my_y, n_y, on_y, lambda k: ot.at[my_y], lambda i: ot.at[i], s_4, r_4)


def all_reduce(matrix, target_part=None, source_part=None):
    n_src = lax.axis_size("src")
    n_tgt = lax.axis_size("tgt")
    size = matrix.size
    lines = -(-size // 128)
    rows = -(-lines // (n_src * 8)) * 8
    flat = jnp.pad(matrix.reshape(-1), (0, n_src * rows * 128 - size)).reshape(n_src, rows, 128)
    vmem = pl.BlockSpec(memory_space=pltpu.VMEM)
    sems = [pltpu.SemaphoreType.DMA((n,)) for n in (n_src, n_src, n_tgt, n_tgt, n_src, n_src)]
    scratch = [pltpu.VMEM((n_src, rows, 128), jnp.float32), pltpu.VMEM((n_tgt, rows, 128), jnp.float32)]
    if target_part is None:
        out = pl.pallas_call(
            functools.partial(all_reduce_kernel, n_src, n_tgt, False),
            out_shape=jax.ShapeDtypeStruct(flat.shape, jnp.float32),
            in_specs=[vmem],
            out_specs=vmem,
            scratch_shapes=scratch + sems,
            compiler_params=pltpu.CompilerParams(collective_id=0, has_side_effects=True),
        )(flat)
        return out.reshape(-1)[:size].reshape(matrix.shape)
    t_rows, width = target_part.shape
    n_y = 4 if n_src % 4 == 0 else n_src
    n_z = n_src // n_y
    piece = t_rows // n_src
    chunks = target_part.astype(jnp.bfloat16).reshape(n_y, n_z, piece, width)
    s_rows = source_part.shape[0]
    pieces = source_part.astype(jnp.bfloat16).reshape(n_tgt, s_rows // n_tgt, width)
    out, target_sum, source_sum = pl.pallas_call(
        functools.partial(all_reduce_kernel, n_src, n_tgt, True),
        out_shape=(jax.ShapeDtypeStruct(flat.shape, jnp.float32),
                   jax.ShapeDtypeStruct(chunks.shape, jnp.bfloat16),
                   jax.ShapeDtypeStruct(pieces.shape[1:], jnp.bfloat16)),
        in_specs=[vmem, vmem, vmem],
        out_specs=(vmem, vmem, vmem),
        scratch_shapes=scratch
        + [pltpu.VMEM(chunks.shape, jnp.bfloat16), pltpu.VMEM((n_z, piece, width), jnp.bfloat16),
           pltpu.VMEM((n_z, piece, width), jnp.bfloat16), pltpu.VMEM(pieces.shape, jnp.bfloat16)]
        + sems
        + [pltpu.SemaphoreType.DMA((n,)) for n in (n_y, n_y, n_z, n_z, n_z, n_z, n_y, n_y, n_tgt, n_tgt)],
        compiler_params=pltpu.CompilerParams(collective_id=1, has_side_effects=True),
    )(flat, chunks, pieces)
    target_sum = target_sum.reshape(t_rows, width)
    return out.reshape(-1)[:size].reshape(matrix.shape), target_sum, source_sum


def stats_gather_kernel(n_src, n_tgt, row_ref, col_ref, row_out, col_out,
                        send_r, recv_r, send_c, recv_c):
    me_s = lax.axis_index("src")
    me_t = lax.axis_index("tgt")
    peer_barrier(n_src, n_tgt)

    def row_copy(k, slot):
        return pltpu.make_async_remote_copy(
            src_ref=row_ref, dst_ref=row_out.at[slot], send_sem=send_r.at[k],
            recv_sem=recv_r.at[slot], device_id=(me_s, k), device_id_type=MESH)

    def col_copy(k, slot):
        return pltpu.make_async_remote_copy(
            src_ref=col_ref, dst_ref=col_out.at[slot], send_sem=send_c.at[k],
            recv_sem=recv_c.at[slot], device_id=(k, me_t), device_id_type=MESH)

    def start_c(d, carry):
        col_copy(lax.rem(me_s + d, n_src), me_s).start()
        return carry
    lax.fori_loop(1, n_src, start_c, 0)

    def start_r(d, carry):
        row_copy(lax.rem(me_t + d, n_tgt), me_t).start()
        return carry
    lax.fori_loop(1, n_tgt, start_r, 0)
    row_out[me_t] = row_ref[...]
    col_out[me_s] = col_ref[...]

    def wait_r(d, carry):
        row_copy(lax.rem(me_t + d, n_tgt), me_t).wait_send()
        j = lax.rem(me_t + n_tgt - d, n_tgt)
        row_copy(j, j).wait_recv()
        return carry
    lax.fori_loop(1, n_tgt, wait_r, 0)

    def wait_c(d, carry):
        col_copy(lax.rem(me_s + d, n_src), me_s).wait_send()
        j = lax.rem(me_s + n_src - d, n_src)
        col_copy(j, j).wait_recv()
        return carry
    lax.fori_loop(1, n_src, wait_c, 0)


def merge(gathered):
    tops, totals = gathered[:, 0], gathered[:, 1]
    best = jnp.max(tops, axis=0)
    return best, jnp.sum(totals * jnp.exp(tops - best[None]), axis=0)


def gather_stats(row_top, row_part, col_top, col_part):
    n_src = lax.axis_size("src")
    n_tgt = lax.axis_size("tgt")
    n_row, n_col = row_top.shape[0], col_top.shape[0]
    rows = jnp.stack([row_top, row_part]).reshape(2 * n_row // 128, 128)
    cols = jnp.stack([col_top, col_part]).reshape(2 * n_col // 128, 128)
    vmem = pl.BlockSpec(memory_space=pltpu.VMEM)
    row_all, col_all = pl.pallas_call(
        functools.partial(stats_gather_kernel, n_src, n_tgt),
        out_shape=(jax.ShapeDtypeStruct((n_tgt,) + rows.shape, jnp.float32),
                   jax.ShapeDtypeStruct((n_src,) + cols.shape, jnp.float32)),
        in_specs=[vmem, vmem],
        out_specs=(vmem, vmem),
        scratch_shapes=[
            pltpu.SemaphoreType.DMA((n_tgt,)),
            pltpu.SemaphoreType.DMA((n_tgt,)),
            pltpu.SemaphoreType.DMA((n_src,)),
            pltpu.SemaphoreType.DMA((n_src,)),
        ],
        compiler_params=pltpu.CompilerParams(collective_id=2, has_side_effects=True),
    )(rows, cols)
    row_top, row_total = merge(row_all.reshape(n_tgt, 2, n_row))
    col_top, col_total = merge(col_all.reshape(n_src, 2, n_col))
    return row_top, row_total, col_top, col_total


def body(source, target, start_map):
    highest = lax.Precision.HIGHEST
    score_scale = 2.0 / math.sqrt(source.shape[1])
    source_f32 = source.astype(jnp.float32)
    target_f32 = target.astype(jnp.float32)
    current = start_map
    for iteration in range(ITERS):
        mapped = jnp.dot(
            source, current.astype(jnp.bfloat16), preferred_element_type=jnp.float32
        ).astype(jnp.bfloat16)
        scores = (
            lax.dot_general(
                mapped, target, (((1,), (1,)), ((), ())), preferred_element_type=jnp.float32
            )
            * score_scale
        )
        row_local = jnp.max(scores, axis=1)
        col_local = jnp.max(scores, axis=0)
        row_part = jnp.sum(jnp.exp(scores - row_local[:, None]), axis=1)
        col_part = jnp.sum(jnp.exp(scores - col_local[None, :]), axis=0)
        row_top, row_total, col_top, col_total = gather_stats(row_local, row_part, col_local, col_part)
        row_weights = (jnp.exp(scores - row_top[:, None]) / row_total[:, None]).astype(jnp.bfloat16)
        col_weights = (jnp.exp(scores - col_top[None, :]) / col_total[None, :]).astype(jnp.bfloat16)
        source_part = jnp.dot(row_weights, target, preferred_element_type=jnp.float32)
        target_part = lax.dot_general(
            col_weights, source, (((0,), (0,)), ((), ())), preferred_element_type=jnp.float32
        )
        covariance = jnp.dot(source_f32.T, source_part, precision=highest)
        covariance = covariance + jnp.dot(target_part.T, target_f32, precision=highest)
        if iteration == ITERS - 1:
            covariance, target_soft, source_soft = all_reduce(covariance, target_part, source_part)
        else:
            covariance = all_reduce(covariance)
        current = polar_steps(covariance)
    return (source_soft, target_soft, current)


def solution(mesh):
    in_specs = (P("src", None), P("tgt", None), P())
    out_specs = (P(("src", "tgt"), None), P("tgt", None), P())
    return jax.shard_map(body, mesh=mesh, in_specs=in_specs, out_specs=out_specs, check_vma=False)
```

```python
import math

import functools

import jax
import jax.numpy as jnp
from jax import lax
from jax.experimental import pallas as pl
from jax.experimental.pallas import tpu as pltpu
from jax.sharding import PartitionSpec as P

MESH = pl.DeviceIdType.MESH

ITERS = 2
NEWTON_STEPS = 8


def polar_steps(covariance):
    highest = lax.Precision.HIGH
    current = covariance / jnp.sqrt(jnp.sum(covariance * covariance) + 1e-06)

    def newton(step, current):
        gram_matrix = jnp.dot(current.T, current, precision=highest)
        return 1.5 * current - 0.5 * jnp.dot(current, gram_matrix, precision=highest)
    return lax.fori_loop(0, NEWTON_STEPS, newton, current)


def polar_value(c):
    highest = lax.Precision.HIGHEST
    norm = jnp.sum(jnp.sum(c * c, axis=1, keepdims=True), axis=0, keepdims=True)
    current = c / jnp.sqrt(norm + 1e-06)

    def newton(step, current):
        outer = lax.dot_general(current, current, (((1,), (1,)), ((), ())),
                                precision=highest, preferred_element_type=jnp.float32)
        return 1.5 * current - 0.5 * jnp.dot(outer, current, precision=highest,
                                              preferred_element_type=jnp.float32)
    return lax.fori_loop(0, NEWTON_STEPS, newton, current)


def peer_barrier(n_src, n_tgt):
    me_s = lax.axis_index("src")
    me_t = lax.axis_index("tgt")
    barrier = pltpu.get_barrier_semaphore()

    def greet_src(d, carry):
        pl.semaphore_signal(barrier, 1, device_id=(lax.rem(me_s + d, n_src), me_t), device_id_type=MESH)
        return carry
    lax.fori_loop(1, n_src, greet_src, 0)

    def greet_tgt(d, carry):
        pl.semaphore_signal(barrier, 1, device_id=(me_s, lax.rem(me_t + d, n_tgt)), device_id_type=MESH)
        return carry
    lax.fori_loop(1, n_tgt, greet_tgt, 0)
    pl.semaphore_wait(barrier, n_src + n_tgt - 2)


def remote(src, dst, send, recv, device):
    return pltpu.make_async_remote_copy(
        src_ref=src, dst_ref=dst, send_sem=send, recv_sem=recv,
        device_id=device, device_id_type=MESH)


def start_all(me, n, device, src, slot, send, recv):
    def step(d, carry):
        k = lax.rem(me + d, n)
        remote(src(k), slot(me), send.at[k], recv.at[me], device(k)).start()
        return carry
    lax.fori_loop(1, n, step, 0)


def wait_all(me, n, device, src, slot, send, recv):
    def step(d, carry):
        k = lax.rem(me + d, n)
        remote(src(k), slot(me), send.at[k], recv.at[me], device(k)).wait_send()
        j = lax.rem(me + n - d, n)
        remote(src(j), slot(j), send.at[j], recv.at[j], device(j)).wait_recv()
        return carry
    lax.fori_loop(1, n, step, 0)


def all_reduce_kernel(n_src, n_tgt, with_target, *refs):
    if with_target:
        (xc, xt, xs, oc, ot, os, op, gather_src, gather_tgt, g1, g2, s1, gs,
         s_a, r_a, s_b, r_b, s_c, r_c, s_1, r_1, s_2, r_2, s_3, r_3, s_4, r_4, s_s, r_s) = refs
    else:
        xc, oc, gather_src, gather_tgt, s_a, r_a, s_b, r_b, s_c, r_c = refs
    me_s = lax.axis_index("src")
    me_t = lax.axis_index("tgt")
    peer_barrier(n_src, n_tgt)
    on_src = lambda k: (k, me_t)
    on_tgt = lambda k: (me_s, k)

    if with_target:
        n_y, n_z = xt.shape[0], xt.shape[1]
        my_z = me_s // n_y
        my_y = me_s % n_y
        on_y = lambda k: (my_z * n_y + k, me_t)
        on_z = lambda k: (k * n_y + my_y, me_t)
        start_all(my_y, n_y, on_y, lambda k: xt.at[k], lambda i: g1.at[i], s_1, r_1)
        start_all(me_t, n_tgt, on_tgt, lambda k: xs.at[k], lambda i: gs.at[i], s_s, r_s)
        g1[my_y] = xt[my_y]
        gs[me_t] = xs[me_t]

    start_all(me_s, n_src, on_src, lambda k: xc.at[k], lambda i: gather_src.at[i], s_a, r_a)
    gather_src[me_s] = xc[me_s]
    wait_all(me_s, n_src, on_src, lambda k: xc.at[k], lambda i: gather_src.at[i], s_a, r_a)
    gather_tgt[me_t] = jnp.sum(gather_src[...], axis=0)

    if with_target:
        wait_all(my_y, n_y, on_y, lambda k: xt.at[k], lambda i: g1.at[i], s_1, r_1)
        s1[...] = jnp.sum(g1[...].astype(jnp.float32), axis=0).astype(s1.dtype)
        start_all(my_z, n_z, on_z, lambda k: s1.at[k], lambda i: g2.at[i], s_2, r_2)
        g2[my_z] = s1[my_z]

    start_all(me_t, n_tgt, on_tgt, lambda k: gather_tgt.at[me_t], lambda i: gather_tgt.at[i], s_b, r_b)
    wait_all(me_t, n_tgt, on_tgt, lambda k: gather_tgt.at[me_t], lambda i: gather_tgt.at[i], s_b, r_b)
    oc[me_s] = jnp.sum(gather_tgt[...], axis=0)
    start_all(me_s, n_src, on_src, lambda k: oc.at[me_s], lambda i: oc.at[i], s_c, r_c)

    if with_target:
        wait_all(my_z, n_z, on_z, lambda k: s1.at[k], lambda i: g2.at[i], s_2, r_2)
        ot[my_y, my_z] = jnp.sum(g2[...].astype(jnp.float32), axis=0).astype(ot.dtype)
        start_all(my_z, n_z, on_z, lambda k: ot.at[my_y, my_z], lambda i: ot.at[my_y, i], s_3, r_3)
    wait_all(me_s, n_src, on_src, lambda k: oc.at[me_s], lambda i: oc.at[i], s_c, r_c)
    if with_target:
        wait_all(my_z, n_z, on_z, lambda k: ot.at[my_y, my_z], lambda i: ot.at[my_y, i], s_3, r_3)
        start_all(my_y, n_y, on_y, lambda k: ot.at[my_y], lambda i: ot.at[i], s_4, r_4)
        width = op.shape[0]
        op[...] = polar_value(oc[...].reshape(-1, width)[:width])
        wait_all(me_t, n_tgt, on_tgt, lambda k: xs.at[k], lambda i: gs.at[i], s_s, r_s)
        os[...] = jnp.sum(gs[...], axis=0).astype(os.dtype)
        wait_all(my_y, n_y, on_y, lambda k: ot.at[my_y], lambda i: ot.at[i], s_4, r_4)


def all_reduce(matrix, target_part=None, source_part=None):
    n_src = lax.axis_size("src")
    n_tgt = lax.axis_size("tgt")
    size = matrix.size
    size_m = matrix.shape[0]
    lines = -(-size // 128)
    rows = -(-lines // (n_src * 8)) * 8
    flat = jnp.pad(matrix.reshape(-1), (0, n_src * rows * 128 - size)).reshape(n_src, rows, 128)
    vmem = pl.BlockSpec(memory_space=pltpu.VMEM)
    sems = [pltpu.SemaphoreType.DMA((n,)) for n in (n_src, n_src, n_tgt, n_tgt, n_src, n_src)]
    scratch = [pltpu.VMEM((n_src, rows, 128), jnp.float32), pltpu.VMEM((n_tgt, rows, 128), jnp.float32)]
    if target_part is None:
        out = pl.pallas_call(
            functools.partial(all_reduce_kernel, n_src, n_tgt, False),
            out_shape=jax.ShapeDtypeStruct(flat.shape, jnp.float32),
            in_specs=[vmem],
            out_specs=vmem,
            scratch_shapes=scratch + sems,
            compiler_params=pltpu.CompilerParams(collective_id=0, has_side_effects=True),
        )(flat)
        return out.reshape(-1)[:size].reshape(matrix.shape)
    t_rows, width = target_part.shape
    n_y = 4 if n_src % 4 == 0 else n_src
    n_z = n_src // n_y
    piece = t_rows // n_src
    chunks = target_part.astype(jnp.bfloat16).reshape(n_y, n_z, piece, width)
    s_rows = source_part.shape[0]
    pieces = source_part.reshape(n_tgt, s_rows // n_tgt, width)
    side = -(-size_m // 128) * 128
    step = -(-side // (n_src * 8)) * 8
    block = jnp.pad(matrix, ((0, n_src * step - size_m), (0, side - size_m))).reshape(n_src, step, side)
    _, target_sum, source_sum, polar = pl.pallas_call(
        functools.partial(all_reduce_kernel, n_src, n_tgt, True),
        out_shape=(jax.ShapeDtypeStruct(block.shape, jnp.float32),
                   jax.ShapeDtypeStruct(chunks.shape, jnp.bfloat16),
                   jax.ShapeDtypeStruct(pieces.shape[1:], jnp.bfloat16),
                   jax.ShapeDtypeStruct((side, side), jnp.float32)),
        in_specs=[vmem, vmem, vmem],
        out_specs=(vmem, vmem, vmem, vmem),
        scratch_shapes=[pltpu.VMEM(block.shape, jnp.float32), pltpu.VMEM((n_tgt, step, side), jnp.float32)]
        + [pltpu.VMEM(chunks.shape, jnp.bfloat16), pltpu.VMEM((n_z, piece, width), jnp.bfloat16),
           pltpu.VMEM((n_z, piece, width), jnp.bfloat16), pltpu.VMEM(pieces.shape, jnp.float32)]
        + sems
        + [pltpu.SemaphoreType.DMA((n,)) for n in (n_y, n_y, n_z, n_z, n_z, n_z, n_y, n_y, n_tgt, n_tgt)],
        compiler_params=pltpu.CompilerParams(collective_id=1, has_side_effects=True),
    )(block, chunks, pieces)
    target_sum = target_sum.reshape(t_rows, width)
    return polar[:size_m, :size_m], target_sum, source_sum


def stats_gather_kernel(n_src, n_tgt, row_ref, col_ref, row_out, col_out,
                        send_r, recv_r, send_c, recv_c):
    me_s = lax.axis_index("src")
    me_t = lax.axis_index("tgt")
    peer_barrier(n_src, n_tgt)

    def row_copy(k, slot):
        return pltpu.make_async_remote_copy(
            src_ref=row_ref, dst_ref=row_out.at[slot], send_sem=send_r.at[k],
            recv_sem=recv_r.at[slot], device_id=(me_s, k), device_id_type=MESH)

    def col_copy(k, slot):
        return pltpu.make_async_remote_copy(
            src_ref=col_ref, dst_ref=col_out.at[slot], send_sem=send_c.at[k],
            recv_sem=recv_c.at[slot], device_id=(k, me_t), device_id_type=MESH)

    def start_c(d, carry):
        col_copy(lax.rem(me_s + d, n_src), me_s).start()
        return carry
    lax.fori_loop(1, n_src, start_c, 0)

    def start_r(d, carry):
        row_copy(lax.rem(me_t + d, n_tgt), me_t).start()
        return carry
    lax.fori_loop(1, n_tgt, start_r, 0)
    row_out[me_t] = row_ref[...]
    col_out[me_s] = col_ref[...]

    def wait_r(d, carry):
        row_copy(lax.rem(me_t + d, n_tgt), me_t).wait_send()
        j = lax.rem(me_t + n_tgt - d, n_tgt)
        row_copy(j, j).wait_recv()
        return carry
    lax.fori_loop(1, n_tgt, wait_r, 0)

    def wait_c(d, carry):
        col_copy(lax.rem(me_s + d, n_src), me_s).wait_send()
        j = lax.rem(me_s + n_src - d, n_src)
        col_copy(j, j).wait_recv()
        return carry
    lax.fori_loop(1, n_src, wait_c, 0)


def merge(gathered):
    tops, totals = gathered[:, 0], gathered[:, 1]
    best = jnp.max(tops, axis=0)
    return best, jnp.sum(totals * jnp.exp(tops - best[None]), axis=0)


def gather_stats(row_top, row_part, col_top, col_part):
    n_src = lax.axis_size("src")
    n_tgt = lax.axis_size("tgt")
    n_row, n_col = row_top.shape[0], col_top.shape[0]
    rows = jnp.stack([row_top, row_part]).reshape(2 * n_row // 128, 128)
    cols = jnp.stack([col_top, col_part]).reshape(2 * n_col // 128, 128)
    vmem = pl.BlockSpec(memory_space=pltpu.VMEM)
    row_all, col_all = pl.pallas_call(
        functools.partial(stats_gather_kernel, n_src, n_tgt),
        out_shape=(jax.ShapeDtypeStruct((n_tgt,) + rows.shape, jnp.float32),
                   jax.ShapeDtypeStruct((n_src,) + cols.shape, jnp.float32)),
        in_specs=[vmem, vmem],
        out_specs=(vmem, vmem),
        scratch_shapes=[
            pltpu.SemaphoreType.DMA((n_tgt,)),
            pltpu.SemaphoreType.DMA((n_tgt,)),
            pltpu.SemaphoreType.DMA((n_src,)),
            pltpu.SemaphoreType.DMA((n_src,)),
        ],
        compiler_params=pltpu.CompilerParams(collective_id=2, has_side_effects=True),
    )(rows, cols)
    row_top, row_total = merge(row_all.reshape(n_tgt, 2, n_row))
    col_top, col_total = merge(col_all.reshape(n_src, 2, n_col))
    return row_top, row_total, col_top, col_total


def body(source, target, start_map):
    highest = lax.Precision.HIGHEST
    score_scale = 2.0 / math.sqrt(source.shape[1])
    source_f32 = source.astype(jnp.float32)
    target_f32 = target.astype(jnp.float32)
    current = start_map
    for iteration in range(ITERS):
        mapped = jnp.dot(
            source, current.astype(jnp.bfloat16), preferred_element_type=jnp.float32
        ).astype(jnp.bfloat16)
        scores = (
            lax.dot_general(
                mapped, target, (((1,), (1,)), ((), ())), preferred_element_type=jnp.float32
            )
            * score_scale
        )
        row_local = jnp.max(scores, axis=1)
        col_local = jnp.max(scores, axis=0)
        row_part = jnp.sum(jnp.exp(scores - row_local[:, None]), axis=1)
        col_part = jnp.sum(jnp.exp(scores - col_local[None, :]), axis=0)
        row_top, row_total, col_top, col_total = gather_stats(row_local, row_part, col_local, col_part)
        row_weights = (jnp.exp(scores - row_top[:, None]) / row_total[:, None]).astype(jnp.bfloat16)
        col_weights = (jnp.exp(scores - col_top[None, :]) / col_total[None, :]).astype(jnp.bfloat16)
        source_part = jnp.dot(row_weights, target, preferred_element_type=jnp.float32)
        target_part = lax.dot_general(
            col_weights, source, (((0,), (0,)), ((), ())), preferred_element_type=jnp.float32
        )
        covariance = jnp.dot(source_f32.T, source_part, precision=highest)
        covariance = covariance + jnp.dot(target_part.T, target_f32, precision=highest)
        if iteration == ITERS - 1:
            current, target_soft, source_soft = all_reduce(covariance, target_part, source_part)
        else:
            current = polar_steps(all_reduce(covariance))
    return (source_soft, target_soft, current)


def solution(mesh):
    in_specs = (P("src", None), P("tgt", None), P())
    out_specs = (P(("src", "tgt"), None), P("tgt", None), P())
    return jax.shard_map(body, mesh=mesh, in_specs=in_specs, out_specs=out_specs, check_vma=False)
```

```python
import math

import functools

import jax
import jax.numpy as jnp
from jax import lax
from jax.experimental import pallas as pl
from jax.experimental.pallas import tpu as pltpu
from jax.sharding import PartitionSpec as P

MESH = pl.DeviceIdType.MESH

ITERS = 2
NEWTON_STEPS = 8


def polar_steps(covariance):
    highest = lax.Precision.HIGH
    current = covariance / jnp.sqrt(jnp.sum(covariance * covariance) + 1e-06)

    def newton(step, current):
        gram_matrix = jnp.dot(current.T, current, precision=highest)
        return 1.5 * current - 0.5 * jnp.dot(current, gram_matrix, precision=highest)
    return lax.fori_loop(0, NEWTON_STEPS, newton, current)


def peer_barrier(n_src, n_tgt):
    me_s = lax.axis_index("src")
    me_t = lax.axis_index("tgt")
    barrier = pltpu.get_barrier_semaphore()

    def greet_src(d, carry):
        pl.semaphore_signal(barrier, 1, device_id=(lax.rem(me_s + d, n_src), me_t), device_id_type=MESH)
        return carry
    lax.fori_loop(1, n_src, greet_src, 0)

    def greet_tgt(d, carry):
        pl.semaphore_signal(barrier, 1, device_id=(me_s, lax.rem(me_t + d, n_tgt)), device_id_type=MESH)
        return carry
    lax.fori_loop(1, n_tgt, greet_tgt, 0)
    pl.semaphore_wait(barrier, n_src + n_tgt - 2)


def remote(src, dst, send, recv, device):
    return pltpu.make_async_remote_copy(
        src_ref=src, dst_ref=dst, send_sem=send, recv_sem=recv,
        device_id=device, device_id_type=MESH)


def start_all(me, n, device, src, slot, send, recv):
    def step(d, carry):
        k = lax.rem(me + d, n)
        remote(src(k), slot(me), send.at[k], recv.at[me], device(k)).start()
        return carry
    lax.fori_loop(1, n, step, 0)


def wait_all(me, n, device, src, slot, send, recv):
    def step(d, carry):
        k = lax.rem(me + d, n)
        remote(src(k), slot(me), send.at[k], recv.at[me], device(k)).wait_send()
        j = lax.rem(me + n - d, n)
        remote(src(j), slot(j), send.at[j], recv.at[j], device(j)).wait_recv()
        return carry
    lax.fori_loop(1, n, step, 0)


def all_reduce_kernel(n_src, n_tgt, with_target, *refs):
    if with_target:
        (xc, xt, xs, oc, ot, os, gather_src, gather_tgt, g1, g2, s1, gs,
         s_a, r_a, s_b, r_b, s_c, r_c, s_1, r_1, s_2, r_2, s_3, r_3, s_4, r_4, s_s, r_s) = refs
    else:
        xc, oc, gather_src, gather_tgt, s_a, r_a, s_b, r_b, s_c, r_c = refs
    me_s = lax.axis_index("src")
    me_t = lax.axis_index("tgt")
    peer_barrier(n_src, n_tgt)
    on_src = lambda k: (k, me_t)
    on_tgt = lambda k: (me_s, k)

    if with_target:
        n_y, n_z = xt.shape[0], xt.shape[1]
        my_z = me_s // n_y
        my_y = me_s % n_y
        on_y = lambda k: (my_z * n_y + k, me_t)
        on_z = lambda k: (k * n_y + my_y, me_t)
        start_all(my_y, n_y, on_y, lambda k: xt.at[k], lambda i: g1.at[i], s_1, r_1)
        start_all(me_t, n_tgt, on_tgt, lambda k: xs.at[k], lambda i: gs.at[i], s_s, r_s)
        g1[my_y] = xt[my_y]
        gs[me_t] = xs[me_t]

    start_all(me_s, n_src, on_src, lambda k: xc.at[k], lambda i: gather_src.at[i], s_a, r_a)
    gather_src[me_s] = xc[me_s]
    wait_all(me_s, n_src, on_src, lambda k: xc.at[k], lambda i: gather_src.at[i], s_a, r_a)
    gather_tgt[me_t] = jnp.sum(gather_src[...], axis=0)

    if with_target:
        wait_all(my_y, n_y, on_y, lambda k: xt.at[k], lambda i: g1.at[i], s_1, r_1)
        s1[...] = jnp.sum(g1[...].astype(jnp.float32), axis=0).astype(s1.dtype)
        start_all(my_z, n_z, on_z, lambda k: s1.at[k], lambda i: g2.at[i], s_2, r_2)
        g2[my_z] = s1[my_z]

    start_all(me_t, n_tgt, on_tgt, lambda k: gather_tgt.at[me_t], lambda i: gather_tgt.at[i], s_b, r_b)
    wait_all(me_t, n_tgt, on_tgt, lambda k: gather_tgt.at[me_t], lambda i: gather_tgt.at[i], s_b, r_b)
    oc[me_s] = jnp.sum(gather_tgt[...], axis=0)
    start_all(me_s, n_src, on_src, lambda k: oc.at[me_s], lambda i: oc.at[i], s_c, r_c)

    if with_target:
        wait_all(my_z, n_z, on_z, lambda k: s1.at[k], lambda i: g2.at[i], s_2, r_2)
        ot[my_y, my_z] = jnp.sum(g2[...].astype(jnp.float32), axis=0).astype(ot.dtype)
        start_all(my_z, n_z, on_z, lambda k: ot.at[my_y, my_z], lambda i: ot.at[my_y, i], s_3, r_3)
    wait_all(me_s, n_src, on_src, lambda k: oc.at[me_s], lambda i: oc.at[i], s_c, r_c)
    if with_target:
        wait_all(my_z, n_z, on_z, lambda k: ot.at[my_y, my_z], lambda i: ot.at[my_y, i], s_3, r_3)
        start_all(my_y, n_y, on_y, lambda k: ot.at[my_y], lambda i: ot.at[i], s_4, r_4)
        wait_all(me_t, n_tgt, on_tgt, lambda k: xs.at[k], lambda i: gs.at[i], s_s, r_s)
        os[...] = jnp.sum(gs[...], axis=0).astype(os.dtype)
        wait_all(my_y, n_y, on_y, lambda k: ot.at[my_y], lambda i: ot.at[i], s_4, r_4)


def all_reduce(matrix, target_part=None, source_part=None):
    n_src = lax.axis_size("src")
    n_tgt = lax.axis_size("tgt")
    size = matrix.size
    lines = -(-size // 128)
    rows = -(-lines // (n_src * 8)) * 8
    flat = jnp.pad(matrix.reshape(-1), (0, n_src * rows * 128 - size)).reshape(n_src, rows, 128)
    vmem = pl.BlockSpec(memory_space=pltpu.VMEM)
    sems = [pltpu.SemaphoreType.DMA((n,)) for n in (n_src, n_src, n_tgt, n_tgt, n_src, n_src)]
    scratch = [pltpu.VMEM((n_src, rows, 128), jnp.float32), pltpu.VMEM((n_tgt, rows, 128), jnp.float32)]
    if target_part is None:
        out = pl.pallas_call(
            functools.partial(all_reduce_kernel, n_src, n_tgt, False),
            out_shape=jax.ShapeDtypeStruct(flat.shape, jnp.float32),
            in_specs=[vmem],
            out_specs=vmem,
            scratch_shapes=scratch + sems,
            compiler_params=pltpu.CompilerParams(collective_id=0, has_side_effects=True),
        )(flat)
        return out.reshape(-1)[:size].reshape(matrix.shape)
    t_rows, width = target_part.shape
    n_y = 4 if n_src % 4 == 0 else n_src
    n_z = n_src // n_y
    piece = t_rows // n_src
    chunks = target_part.astype(jnp.bfloat16).reshape(n_y, n_z, piece, width)
    s_rows = source_part.shape[0]
    pieces = source_part.reshape(n_tgt, s_rows // n_tgt, width)
    out, target_sum, source_sum = pl.pallas_call(
        functools.partial(all_reduce_kernel, n_src, n_tgt, True),
        out_shape=(jax.ShapeDtypeStruct(flat.shape, jnp.float32),
                   jax.ShapeDtypeStruct(chunks.shape, jnp.bfloat16),
                   jax.ShapeDtypeStruct(pieces.shape[1:], jnp.bfloat16)),
        in_specs=[vmem, vmem, vmem],
        out_specs=(vmem, vmem, vmem),
        scratch_shapes=scratch
        + [pltpu.VMEM(chunks.shape, jnp.bfloat16), pltpu.VMEM((n_z, piece, width), jnp.bfloat16),
           pltpu.VMEM((n_z, piece, width), jnp.bfloat16), pltpu.VMEM(pieces.shape, jnp.float32)]
        + sems
        + [pltpu.SemaphoreType.DMA((n,)) for n in (n_y, n_y, n_z, n_z, n_z, n_z, n_y, n_y, n_tgt, n_tgt)],
        compiler_params=pltpu.CompilerParams(collective_id=1, has_side_effects=True),
    )(flat, chunks, pieces)
    target_sum = target_sum.reshape(t_rows, width)
    return out.reshape(-1)[:size].reshape(matrix.shape), target_sum, source_sum


def stats_gather_kernel(n_src, n_tgt, row_ref, col_ref, row_out, col_out,
                        send_r, recv_r, send_c, recv_c):
    me_s = lax.axis_index("src")
    me_t = lax.axis_index("tgt")
    peer_barrier(n_src, n_tgt)

    def row_copy(k, slot):
        return pltpu.make_async_remote_copy(
            src_ref=row_ref, dst_ref=row_out.at[slot], send_sem=send_r.at[k],
            recv_sem=recv_r.at[slot], device_id=(me_s, k), device_id_type=MESH)

    def col_copy(k, slot):
        return pltpu.make_async_remote_copy(
            src_ref=col_ref, dst_ref=col_out.at[slot], send_sem=send_c.at[k],
            recv_sem=recv_c.at[slot], device_id=(k, me_t), device_id_type=MESH)

    def start_c(d, carry):
        col_copy(lax.rem(me_s + d, n_src), me_s).start()
        return carry
    lax.fori_loop(1, n_src, start_c, 0)

    def start_r(d, carry):
        row_copy(lax.rem(me_t + d, n_tgt), me_t).start()
        return carry
    lax.fori_loop(1, n_tgt, start_r, 0)
    row_out[me_t] = row_ref[...]
    col_out[me_s] = col_ref[...]

    def wait_r(d, carry):
        row_copy(lax.rem(me_t + d, n_tgt), me_t).wait_send()
        j = lax.rem(me_t + n_tgt - d, n_tgt)
        row_copy(j, j).wait_recv()
        return carry
    lax.fori_loop(1, n_tgt, wait_r, 0)

    def wait_c(d, carry):
        col_copy(lax.rem(me_s + d, n_src), me_s).wait_send()
        j = lax.rem(me_s + n_src - d, n_src)
        col_copy(j, j).wait_recv()
        return carry
    lax.fori_loop(1, n_src, wait_c, 0)


def merge(gathered):
    tops, totals = gathered[:, 0], gathered[:, 1]
    best = jnp.max(tops, axis=0)
    return best, jnp.sum(totals * jnp.exp(tops - best[None]), axis=0)


def gather_stats(row_top, row_part, col_top, col_part):
    n_src = lax.axis_size("src")
    n_tgt = lax.axis_size("tgt")
    n_row, n_col = row_top.shape[0], col_top.shape[0]
    rows = jnp.stack([row_top, row_part]).reshape(2 * n_row // 128, 128)
    cols = jnp.stack([col_top, col_part]).reshape(2 * n_col // 128, 128)
    vmem = pl.BlockSpec(memory_space=pltpu.VMEM)
    row_all, col_all = pl.pallas_call(
        functools.partial(stats_gather_kernel, n_src, n_tgt),
        out_shape=(jax.ShapeDtypeStruct((n_tgt,) + rows.shape, jnp.float32),
                   jax.ShapeDtypeStruct((n_src,) + cols.shape, jnp.float32)),
        in_specs=[vmem, vmem],
        out_specs=(vmem, vmem),
        scratch_shapes=[
            pltpu.SemaphoreType.DMA((n_tgt,)),
            pltpu.SemaphoreType.DMA((n_tgt,)),
            pltpu.SemaphoreType.DMA((n_src,)),
            pltpu.SemaphoreType.DMA((n_src,)),
        ],
        compiler_params=pltpu.CompilerParams(collective_id=2, has_side_effects=True),
    )(rows, cols)
    row_top, row_total = merge(row_all.reshape(n_tgt, 2, n_row))
    col_top, col_total = merge(col_all.reshape(n_src, 2, n_col))
    return row_top, row_total, col_top, col_total


def body(source, target, start_map):
    highest = lax.Precision.HIGHEST
    score_scale = 2.0 / math.sqrt(source.shape[1])
    source_f32 = source.astype(jnp.float32)
    target_f32 = target.astype(jnp.float32)
    current = start_map
    for iteration in range(ITERS):
        mapped = jnp.dot(
            source, current.astype(jnp.bfloat16), preferred_element_type=jnp.float32
        ).astype(jnp.bfloat16)
        scores = (
            lax.dot_general(
                mapped, target, (((1,), (1,)), ((), ())), preferred_element_type=jnp.float32
            )
            * score_scale
        )
        row_local = jnp.max(scores, axis=1)
        col_local = jnp.max(scores, axis=0)
        row_part = jnp.sum(jnp.exp(scores - row_local[:, None]), axis=1)
        col_part = jnp.sum(jnp.exp(scores - col_local[None, :]), axis=0)
        row_top, row_total, col_top, col_total = gather_stats(row_local, row_part, col_local, col_part)
        row_weights = (jnp.exp(scores - row_top[:, None]) / row_total[:, None]).astype(jnp.bfloat16)
        col_weights = (jnp.exp(scores - col_top[None, :]) / col_total[None, :]).astype(jnp.bfloat16)
        source_part = jnp.dot(row_weights, target, preferred_element_type=jnp.float32)
        target_part = lax.dot_general(
            col_weights, source, (((0,), (0,)), ((), ())), preferred_element_type=jnp.float32
        )
        covariance = jnp.dot(source_f32.T, source_part, precision=lax.Precision.HIGH)
        covariance = covariance + jnp.dot(target_part.T, target_f32, precision=lax.Precision.HIGH)
        if iteration == ITERS - 1:
            covariance, target_soft, source_soft = all_reduce(covariance, target_part, source_part)
        else:
            covariance = all_reduce(covariance)
        current = polar_steps(covariance)
    return (source_soft, target_soft, current)


def solution(mesh):
    in_specs = (P("src", None), P("tgt", None), P())
    out_specs = (P(("src", "tgt"), None), P("tgt", None), P())
    return jax.shard_map(body, mesh=mesh, in_specs=in_specs, out_specs=out_specs, check_vma=False)
```

```python
import math

import functools

import jax
import jax.numpy as jnp
from jax import lax
from jax.experimental import pallas as pl
from jax.experimental.pallas import tpu as pltpu
from jax.sharding import PartitionSpec as P

MESH = pl.DeviceIdType.MESH

ITERS = 2
NEWTON_STEPS = 8


def polar_steps(covariance):
    highest = lax.Precision.HIGH
    current = covariance / jnp.sqrt(jnp.sum(covariance * covariance) + 1e-06)

    def newton(step, current):
        gram_matrix = jnp.dot(current.T, current, precision=highest)
        return 1.5 * current - 0.5 * jnp.dot(current, gram_matrix, precision=highest)
    return lax.fori_loop(0, NEWTON_STEPS, newton, current, unroll=2)


def peer_barrier(n_src, n_tgt):
    me_s = lax.axis_index("src")
    me_t = lax.axis_index("tgt")
    barrier = pltpu.get_barrier_semaphore()

    def greet_src(d, carry):
        pl.semaphore_signal(barrier, 1, device_id=(lax.rem(me_s + d, n_src), me_t), device_id_type=MESH)
        return carry
    lax.fori_loop(1, n_src, greet_src, 0)

    def greet_tgt(d, carry):
        pl.semaphore_signal(barrier, 1, device_id=(me_s, lax.rem(me_t + d, n_tgt)), device_id_type=MESH)
        return carry
    lax.fori_loop(1, n_tgt, greet_tgt, 0)
    pl.semaphore_wait(barrier, n_src + n_tgt - 2)


def remote(src, dst, send, recv, device):
    return pltpu.make_async_remote_copy(
        src_ref=src, dst_ref=dst, send_sem=send, recv_sem=recv,
        device_id=device, device_id_type=MESH)


def start_all(me, n, device, src, slot, send, recv):
    def step(d, carry):
        k = lax.rem(me + d, n)
        remote(src(k), slot(me), send.at[k], recv.at[me], device(k)).start()
        return carry
    lax.fori_loop(1, n, step, 0)


def wait_all(me, n, device, src, slot, send, recv):
    def step(d, carry):
        k = lax.rem(me + d, n)
        remote(src(k), slot(me), send.at[k], recv.at[me], device(k)).wait_send()
        j = lax.rem(me + n - d, n)
        remote(src(j), slot(j), send.at[j], recv.at[j], device(j)).wait_recv()
        return carry
    lax.fori_loop(1, n, step, 0)


def all_reduce_kernel(n_src, n_tgt, with_target, *refs):
    if with_target:
        (xc, xt, xs, oc, ot, os, gather_src, gather_tgt, g1, g2, s1, gs,
         s_a, r_a, s_b, r_b, s_c, r_c, s_1, r_1, s_2, r_2, s_3, r_3, s_4, r_4, s_s, r_s) = refs
    else:
        xc, oc, gather_src, gather_tgt, s_a, r_a, s_b, r_b, s_c, r_c = refs
    me_s = lax.axis_index("src")
    me_t = lax.axis_index("tgt")
    peer_barrier(n_src, n_tgt)
    on_src = lambda k: (k, me_t)
    on_tgt = lambda k: (me_s, k)

    if with_target:
        n_y, n_z = xt.shape[0], xt.shape[1]
        my_z = me_s // n_y
        my_y = me_s % n_y
        on_y = lambda k: (my_z * n_y + k, me_t)
        on_z = lambda k: (k * n_y + my_y, me_t)
        start_all(my_y, n_y, on_y, lambda k: xt.at[k], lambda i: g1.at[i], s_1, r_1)
        start_all(me_t, n_tgt, on_tgt, lambda k: xs.at[k], lambda i: gs.at[i], s_s, r_s)
        g1[my_y] = xt[my_y]
        gs[me_t] = xs[me_t]

    start_all(me_s, n_src, on_src, lambda k: xc.at[k], lambda i: gather_src.at[i], s_a, r_a)
    gather_src[me_s] = xc[me_s]
    wait_all(me_s, n_src, on_src, lambda k: xc.at[k], lambda i: gather_src.at[i], s_a, r_a)
    gather_tgt[me_t] = jnp.sum(gather_src[...], axis=0)

    if with_target:
        wait_all(my_y, n_y, on_y, lambda k: xt.at[k], lambda i: g1.at[i], s_1, r_1)
        s1[...] = jnp.sum(g1[...].astype(jnp.float32), axis=0).astype(s1.dtype)
        start_all(my_z, n_z, on_z, lambda k: s1.at[k], lambda i: g2.at[i], s_2, r_2)
        g2[my_z] = s1[my_z]

    start_all(me_t, n_tgt, on_tgt, lambda k: gather_tgt.at[me_t], lambda i: gather_tgt.at[i], s_b, r_b)
    wait_all(me_t, n_tgt, on_tgt, lambda k: gather_tgt.at[me_t], lambda i: gather_tgt.at[i], s_b, r_b)
    oc[me_s] = jnp.sum(gather_tgt[...], axis=0)
    start_all(me_s, n_src, on_src, lambda k: oc.at[me_s], lambda i: oc.at[i], s_c, r_c)

    if with_target:
        wait_all(my_z, n_z, on_z, lambda k: s1.at[k], lambda i: g2.at[i], s_2, r_2)
        ot[my_y, my_z] = jnp.sum(g2[...].astype(jnp.float32), axis=0).astype(ot.dtype)
        start_all(my_z, n_z, on_z, lambda k: ot.at[my_y, my_z], lambda i: ot.at[my_y, i], s_3, r_3)
    wait_all(me_s, n_src, on_src, lambda k: oc.at[me_s], lambda i: oc.at[i], s_c, r_c)
    if with_target:
        wait_all(my_z, n_z, on_z, lambda k: ot.at[my_y, my_z], lambda i: ot.at[my_y, i], s_3, r_3)
        start_all(my_y, n_y, on_y, lambda k: ot.at[my_y], lambda i: ot.at[i], s_4, r_4)
        wait_all(me_t, n_tgt, on_tgt, lambda k: xs.at[k], lambda i: gs.at[i], s_s, r_s)
        os[...] = jnp.sum(gs[...], axis=0).astype(os.dtype)
        wait_all(my_y, n_y, on_y, lambda k: ot.at[my_y], lambda i: ot.at[i], s_4, r_4)


def all_reduce(matrix, target_part=None, source_part=None):
    n_src = lax.axis_size("src")
    n_tgt = lax.axis_size("tgt")
    size = matrix.size
    lines = -(-size // 128)
    rows = -(-lines // (n_src * 8)) * 8
    flat = jnp.pad(matrix.reshape(-1), (0, n_src * rows * 128 - size)).reshape(n_src, rows, 128)
    vmem = pl.BlockSpec(memory_space=pltpu.VMEM)
    sems = [pltpu.SemaphoreType.DMA((n,)) for n in (n_src, n_src, n_tgt, n_tgt, n_src, n_src)]
    scratch = [pltpu.VMEM((n_src, rows, 128), jnp.float32), pltpu.VMEM((n_tgt, rows, 128), jnp.float32)]
    if target_part is None:
        out = pl.pallas_call(
            functools.partial(all_reduce_kernel, n_src, n_tgt, False),
            out_shape=jax.ShapeDtypeStruct(flat.shape, jnp.float32),
            in_specs=[vmem],
            out_specs=vmem,
            scratch_shapes=scratch + sems,
            compiler_params=pltpu.CompilerParams(collective_id=0, has_side_effects=True),
        )(flat)
        return out.reshape(-1)[:size].reshape(matrix.shape)
    t_rows, width = target_part.shape
    n_y = 4 if n_src % 4 == 0 else n_src
    n_z = n_src // n_y
    piece = t_rows // n_src
    chunks = target_part.astype(jnp.bfloat16).reshape(n_y, n_z, piece, width)
    s_rows = source_part.shape[0]
    pieces = source_part.reshape(n_tgt, s_rows // n_tgt, width)
    out, target_sum, source_sum = pl.pallas_call(
        functools.partial(all_reduce_kernel, n_src, n_tgt, True),
        out_shape=(jax.ShapeDtypeStruct(flat.shape, jnp.float32),
                   jax.ShapeDtypeStruct(chunks.shape, jnp.bfloat16),
                   jax.ShapeDtypeStruct(pieces.shape[1:], jnp.bfloat16)),
        in_specs=[vmem, vmem, vmem],
        out_specs=(vmem, vmem, vmem),
        scratch_shapes=scratch
        + [pltpu.VMEM(chunks.shape, jnp.bfloat16), pltpu.VMEM((n_z, piece, width), jnp.bfloat16),
           pltpu.VMEM((n_z, piece, width), jnp.bfloat16), pltpu.VMEM(pieces.shape, jnp.float32)]
        + sems
        + [pltpu.SemaphoreType.DMA((n,)) for n in (n_y, n_y, n_z, n_z, n_z, n_z, n_y, n_y, n_tgt, n_tgt)],
        compiler_params=pltpu.CompilerParams(collective_id=1, has_side_effects=True),
    )(flat, chunks, pieces)
    target_sum = target_sum.reshape(t_rows, width)
    return out.reshape(-1)[:size].reshape(matrix.shape), target_sum, source_sum


def stats_gather_kernel(n_src, n_tgt, row_ref, col_ref, row_out, col_out,
                        send_r, recv_r, send_c, recv_c):
    me_s = lax.axis_index("src")
    me_t = lax.axis_index("tgt")
    peer_barrier(n_src, n_tgt)

    def row_copy(k, slot):
        return pltpu.make_async_remote_copy(
            src_ref=row_ref, dst_ref=row_out.at[slot], send_sem=send_r.at[k],
            recv_sem=recv_r.at[slot], device_id=(me_s, k), device_id_type=MESH)

    def col_copy(k, slot):
        return pltpu.make_async_remote_copy(
            src_ref=col_ref, dst_ref=col_out.at[slot], send_sem=send_c.at[k],
            recv_sem=recv_c.at[slot], device_id=(k, me_t), device_id_type=MESH)

    def start_c(d, carry):
        col_copy(lax.rem(me_s + d, n_src), me_s).start()
        return carry
    lax.fori_loop(1, n_src, start_c, 0)

    def start_r(d, carry):
        row_copy(lax.rem(me_t + d, n_tgt), me_t).start()
        return carry
    lax.fori_loop(1, n_tgt, start_r, 0)
    row_out[me_t] = row_ref[...]
    col_out[me_s] = col_ref[...]

    def wait_r(d, carry):
        row_copy(lax.rem(me_t + d, n_tgt), me_t).wait_send()
        j = lax.rem(me_t + n_tgt - d, n_tgt)
        row_copy(j, j).wait_recv()
        return carry
    lax.fori_loop(1, n_tgt, wait_r, 0)

    def wait_c(d, carry):
        col_copy(lax.rem(me_s + d, n_src), me_s).wait_send()
        j = lax.rem(me_s + n_src - d, n_src)
        col_copy(j, j).wait_recv()
        return carry
    lax.fori_loop(1, n_src, wait_c, 0)


def merge(gathered):
    tops, totals = gathered[:, 0], gathered[:, 1]
    best = jnp.max(tops, axis=0)
    return best, jnp.sum(totals * jnp.exp(tops - best[None]), axis=0)


def gather_stats(row_top, row_part, col_top, col_part):
    n_src = lax.axis_size("src")
    n_tgt = lax.axis_size("tgt")
    n_row, n_col = row_top.shape[0], col_top.shape[0]
    rows = jnp.stack([row_top, row_part]).reshape(2 * n_row // 128, 128)
    cols = jnp.stack([col_top, col_part]).reshape(2 * n_col // 128, 128)
    vmem = pl.BlockSpec(memory_space=pltpu.VMEM)
    row_all, col_all = pl.pallas_call(
        functools.partial(stats_gather_kernel, n_src, n_tgt),
        out_shape=(jax.ShapeDtypeStruct((n_tgt,) + rows.shape, jnp.float32),
                   jax.ShapeDtypeStruct((n_src,) + cols.shape, jnp.float32)),
        in_specs=[vmem, vmem],
        out_specs=(vmem, vmem),
        scratch_shapes=[
            pltpu.SemaphoreType.DMA((n_tgt,)),
            pltpu.SemaphoreType.DMA((n_tgt,)),
            pltpu.SemaphoreType.DMA((n_src,)),
            pltpu.SemaphoreType.DMA((n_src,)),
        ],
        compiler_params=pltpu.CompilerParams(collective_id=2, has_side_effects=True),
    )(rows, cols)
    row_top, row_total = merge(row_all.reshape(n_tgt, 2, n_row))
    col_top, col_total = merge(col_all.reshape(n_src, 2, n_col))
    return row_top, row_total, col_top, col_total


def body(source, target, start_map):
    highest = lax.Precision.HIGHEST
    score_scale = 2.0 / math.sqrt(source.shape[1])
    source_f32 = source.astype(jnp.float32)
    target_f32 = target.astype(jnp.float32)
    current = start_map
    for iteration in range(ITERS):
        mapped = jnp.dot(
            source, current.astype(jnp.bfloat16), preferred_element_type=jnp.float32
        ).astype(jnp.bfloat16)
        scores = (
            lax.dot_general(
                mapped, target, (((1,), (1,)), ((), ())), preferred_element_type=jnp.float32
            )
            * score_scale
        )
        row_local = jnp.max(scores, axis=1)
        col_local = jnp.max(scores, axis=0)
        row_part = jnp.sum(jnp.exp(scores - row_local[:, None]), axis=1)
        col_part = jnp.sum(jnp.exp(scores - col_local[None, :]), axis=0)
        row_top, row_total, col_top, col_total = gather_stats(row_local, row_part, col_local, col_part)
        row_weights = (jnp.exp(scores - row_top[:, None]) / row_total[:, None]).astype(jnp.bfloat16)
        col_weights = (jnp.exp(scores - col_top[None, :]) / col_total[None, :]).astype(jnp.bfloat16)
        source_part = jnp.dot(row_weights, target, preferred_element_type=jnp.float32)
        target_part = lax.dot_general(
            col_weights, source, (((0,), (0,)), ((), ())), preferred_element_type=jnp.float32
        )
        covariance = jnp.dot(source_f32.T, source_part, precision=lax.Precision.HIGH)
        covariance = covariance + jnp.dot(target_part.T, target_f32, precision=lax.Precision.HIGH)
        if iteration == ITERS - 1:
            covariance, target_soft, source_soft = all_reduce(covariance, target_part, source_part)
        else:
            covariance = all_reduce(covariance)
        current = polar_steps(covariance)
    return (source_soft, target_soft, current)


def solution(mesh):
    in_specs = (P("src", None), P("tgt", None), P())
    out_specs = (P(("src", "tgt"), None), P("tgt", None), P())
    return jax.shard_map(body, mesh=mesh, in_specs=in_specs, out_specs=out_specs, check_vma=False)
```

```python
import math

import functools

import jax
import jax.numpy as jnp
from jax import lax
from jax.experimental import pallas as pl
from jax.experimental.pallas import tpu as pltpu
from jax.sharding import PartitionSpec as P

MESH = pl.DeviceIdType.MESH

ITERS = 2
NEWTON_STEPS = 8


def polar_steps(covariance):
    highest = lax.Precision.HIGH
    current = covariance / jnp.sqrt(jnp.sum(covariance * covariance) + 1e-06)

    def newton(step, current):
        gram_matrix = jnp.dot(current.T, current, precision=highest)
        return 1.5 * current - 0.5 * jnp.dot(current, gram_matrix, precision=highest)
    return lax.fori_loop(0, NEWTON_STEPS, newton, current, unroll=2)


def peer_barrier(n_src, n_tgt):
    me_s = lax.axis_index("src")
    me_t = lax.axis_index("tgt")
    barrier = pltpu.get_barrier_semaphore()

    def greet_src(d, carry):
        pl.semaphore_signal(barrier, 1, device_id=(lax.rem(me_s + d, n_src), me_t), device_id_type=MESH)
        return carry
    lax.fori_loop(1, n_src, greet_src, 0)

    def greet_tgt(d, carry):
        pl.semaphore_signal(barrier, 1, device_id=(me_s, lax.rem(me_t + d, n_tgt)), device_id_type=MESH)
        return carry
    lax.fori_loop(1, n_tgt, greet_tgt, 0)
    pl.semaphore_wait(barrier, n_src + n_tgt - 2)


def remote(src, dst, send, recv, device):
    return pltpu.make_async_remote_copy(
        src_ref=src, dst_ref=dst, send_sem=send, recv_sem=recv,
        device_id=device, device_id_type=MESH)


def start_all(me, n, device, src, slot, send, recv):
    def step(d, carry):
        k = lax.rem(me + d, n)
        remote(src(k), slot(me), send.at[k], recv.at[me], device(k)).start()
        return carry
    lax.fori_loop(1, n, step, 0)


def wait_all(me, n, device, src, slot, send, recv):
    def step(d, carry):
        k = lax.rem(me + d, n)
        remote(src(k), slot(me), send.at[k], recv.at[me], device(k)).wait_send()
        j = lax.rem(me + n - d, n)
        remote(src(j), slot(j), send.at[j], recv.at[j], device(j)).wait_recv()
        return carry
    lax.fori_loop(1, n, step, 0)


def all_reduce_kernel(n_src, n_tgt, with_target, *refs):
    if with_target:
        (xc, xt, xs, oc, ot, os, gather_src, gather_tgt, g1, g2, s1, gs,
         s_a, r_a, s_b, r_b, s_c, r_c, s_1, r_1, s_2, r_2, s_3, r_3, s_4, r_4, s_s, r_s) = refs
    else:
        xc, oc, gather_src, gather_tgt, s_a, r_a, s_b, r_b, s_c, r_c = refs
    me_s = lax.axis_index("src")
    me_t = lax.axis_index("tgt")
    peer_barrier(n_src, n_tgt)
    on_src = lambda k: (k, me_t)
    on_tgt = lambda k: (me_s, k)

    if with_target:
        n_y, n_z = xt.shape[0], xt.shape[1]
        my_z = me_s // n_y
        my_y = me_s % n_y
        on_y = lambda k: (my_z * n_y + k, me_t)
        on_z = lambda k: (k * n_y + my_y, me_t)
        start_all(my_y, n_y, on_y, lambda k: xt.at[k], lambda i: g1.at[i], s_1, r_1)
        start_all(me_t, n_tgt, on_tgt, lambda k: xs.at[k], lambda i: gs.at[i], s_s, r_s)
        g1[my_y] = xt[my_y]
        gs[me_t] = xs[me_t]

    start_all(me_s, n_src, on_src, lambda k: xc.at[k], lambda i: gather_src.at[i], s_a, r_a)
    gather_src[me_s] = xc[me_s]
    wait_all(me_s, n_src, on_src, lambda k: xc.at[k], lambda i: gather_src.at[i], s_a, r_a)
    gather_tgt[me_t] = jnp.sum(gather_src[...], axis=0)

    if with_target:
        wait_all(my_y, n_y, on_y, lambda k: xt.at[k], lambda i: g1.at[i], s_1, r_1)
        s1[...] = jnp.sum(g1[...].astype(jnp.float32), axis=0).astype(s1.dtype)
        start_all(my_z, n_z, on_z, lambda k: s1.at[k], lambda i: g2.at[i], s_2, r_2)
        g2[my_z] = s1[my_z]

    start_all(me_t, n_tgt, on_tgt, lambda k: gather_tgt.at[me_t], lambda i: gather_tgt.at[i], s_b, r_b)
    wait_all(me_t, n_tgt, on_tgt, lambda k: gather_tgt.at[me_t], lambda i: gather_tgt.at[i], s_b, r_b)
    oc[me_s] = jnp.sum(gather_tgt[...], axis=0)
    start_all(me_s, n_src, on_src, lambda k: oc.at[me_s], lambda i: oc.at[i], s_c, r_c)

    if with_target:
        wait_all(my_z, n_z, on_z, lambda k: s1.at[k], lambda i: g2.at[i], s_2, r_2)
        ot[my_y, my_z] = jnp.sum(g2[...].astype(jnp.float32), axis=0).astype(ot.dtype)
        start_all(my_z, n_z, on_z, lambda k: ot.at[my_y, my_z], lambda i: ot.at[my_y, i], s_3, r_3)
    wait_all(me_s, n_src, on_src, lambda k: oc.at[me_s], lambda i: oc.at[i], s_c, r_c)
    if with_target:
        wait_all(my_z, n_z, on_z, lambda k: ot.at[my_y, my_z], lambda i: ot.at[my_y, i], s_3, r_3)
        start_all(my_y, n_y, on_y, lambda k: ot.at[my_y], lambda i: ot.at[i], s_4, r_4)
        wait_all(me_t, n_tgt, on_tgt, lambda k: xs.at[k], lambda i: gs.at[i], s_s, r_s)
        os[...] = jnp.sum(gs[...], axis=0).astype(os.dtype)
        wait_all(my_y, n_y, on_y, lambda k: ot.at[my_y], lambda i: ot.at[i], s_4, r_4)


def all_reduce(matrix, target_part=None, source_part=None):
    n_src = lax.axis_size("src")
    n_tgt = lax.axis_size("tgt")
    size = matrix.size
    lines = -(-size // 128)
    rows = -(-lines // (n_src * 8)) * 8
    flat = jnp.pad(matrix.reshape(-1), (0, n_src * rows * 128 - size)).reshape(n_src, rows, 128)
    vmem = pl.BlockSpec(memory_space=pltpu.VMEM)
    sems = [pltpu.SemaphoreType.DMA((n,)) for n in (n_src, n_src, n_tgt, n_tgt, n_src, n_src)]
    scratch = [pltpu.VMEM((n_src, rows, 128), jnp.float32), pltpu.VMEM((n_tgt, rows, 128), jnp.float32)]
    if target_part is None:
        out = pl.pallas_call(
            functools.partial(all_reduce_kernel, n_src, n_tgt, False),
            out_shape=jax.ShapeDtypeStruct(flat.shape, jnp.float32),
            in_specs=[vmem],
            out_specs=vmem,
            scratch_shapes=scratch + sems,
            compiler_params=pltpu.CompilerParams(collective_id=0, has_side_effects=True),
        )(flat)
        return out.reshape(-1)[:size].reshape(matrix.shape)
    t_rows, width = target_part.shape
    n_y = 4 if n_src % 4 == 0 else n_src
    n_z = n_src // n_y
    piece = t_rows // n_src
    chunks = target_part.astype(jnp.bfloat16).reshape(n_y, n_z, piece, width)
    s_rows = source_part.shape[0]
    pieces = source_part.reshape(n_tgt, s_rows // n_tgt, width)
    out, target_sum, source_sum = pl.pallas_call(
        functools.partial(all_reduce_kernel, n_src, n_tgt, True),
        out_shape=(jax.ShapeDtypeStruct(flat.shape, jnp.float32),
                   jax.ShapeDtypeStruct(chunks.shape, jnp.bfloat16),
                   jax.ShapeDtypeStruct(pieces.shape[1:], jnp.bfloat16)),
        in_specs=[vmem, vmem, vmem],
        out_specs=(vmem, vmem, vmem),
        scratch_shapes=scratch
        + [pltpu.VMEM(chunks.shape, jnp.bfloat16), pltpu.VMEM((n_z, piece, width), jnp.bfloat16),
           pltpu.VMEM((n_z, piece, width), jnp.bfloat16), pltpu.VMEM(pieces.shape, jnp.float32)]
        + sems
        + [pltpu.SemaphoreType.DMA((n,)) for n in (n_y, n_y, n_z, n_z, n_z, n_z, n_y, n_y, n_tgt, n_tgt)],
        compiler_params=pltpu.CompilerParams(collective_id=1, has_side_effects=True),
    )(flat, chunks, pieces)
    target_sum = target_sum.reshape(t_rows, width)
    return out.reshape(-1)[:size].reshape(matrix.shape), target_sum, source_sum


def stats_gather_kernel(n_src, n_tgt, row_ref, col_ref, row_out, col_out,
                        send_r, recv_r, send_c, recv_c):
    me_s = lax.axis_index("src")
    me_t = lax.axis_index("tgt")
    peer_barrier(n_src, n_tgt)

    def row_copy(k, slot):
        return pltpu.make_async_remote_copy(
            src_ref=row_ref, dst_ref=row_out.at[slot], send_sem=send_r.at[k],
            recv_sem=recv_r.at[slot], device_id=(me_s, k), device_id_type=MESH)

    def col_copy(k, slot):
        return pltpu.make_async_remote_copy(
            src_ref=col_ref, dst_ref=col_out.at[slot], send_sem=send_c.at[k],
            recv_sem=recv_c.at[slot], device_id=(k, me_t), device_id_type=MESH)

    def start_c(d, carry):
        col_copy(lax.rem(me_s + d, n_src), me_s).start()
        return carry
    lax.fori_loop(1, n_src, start_c, 0)

    def start_r(d, carry):
        row_copy(lax.rem(me_t + d, n_tgt), me_t).start()
        return carry
    lax.fori_loop(1, n_tgt, start_r, 0)
    row_out[me_t] = row_ref[...]
    col_out[me_s] = col_ref[...]

    def wait_r(d, carry):
        row_copy(lax.rem(me_t + d, n_tgt), me_t).wait_send()
        j = lax.rem(me_t + n_tgt - d, n_tgt)
        row_copy(j, j).wait_recv()
        return carry
    lax.fori_loop(1, n_tgt, wait_r, 0)

    def wait_c(d, carry):
        col_copy(lax.rem(me_s + d, n_src), me_s).wait_send()
        j = lax.rem(me_s + n_src - d, n_src)
        col_copy(j, j).wait_recv()
        return carry
    lax.fori_loop(1, n_src, wait_c, 0)


def merge(gathered):
    tops, totals = gathered[:, 0], gathered[:, 1]
    best = jnp.max(tops, axis=0)
    return best, jnp.sum(totals * jnp.exp(tops - best[None]), axis=0)


def gather_stats(row_top, row_part, col_top, col_part):
    n_src = lax.axis_size("src")
    n_tgt = lax.axis_size("tgt")
    n_row, n_col = row_top.shape[0], col_top.shape[0]
    rows = jnp.stack([row_top, row_part]).reshape(2 * n_row // 128, 128)
    cols = jnp.stack([col_top, col_part]).reshape(2 * n_col // 128, 128)
    vmem = pl.BlockSpec(memory_space=pltpu.VMEM)
    row_all, col_all = pl.pallas_call(
        functools.partial(stats_gather_kernel, n_src, n_tgt),
        out_shape=(jax.ShapeDtypeStruct((n_tgt,) + rows.shape, jnp.float32),
                   jax.ShapeDtypeStruct((n_src,) + cols.shape, jnp.float32)),
        in_specs=[vmem, vmem],
        out_specs=(vmem, vmem),
        scratch_shapes=[
            pltpu.SemaphoreType.DMA((n_tgt,)),
            pltpu.SemaphoreType.DMA((n_tgt,)),
            pltpu.SemaphoreType.DMA((n_src,)),
            pltpu.SemaphoreType.DMA((n_src,)),
        ],
        compiler_params=pltpu.CompilerParams(collective_id=2, has_side_effects=True),
    )(rows, cols)
    row_top, row_total = merge(row_all.reshape(n_tgt, 2, n_row))
    col_top, col_total = merge(col_all.reshape(n_src, 2, n_col))
    return row_top, row_total, col_top, col_total


def body(source, target, start_map):
    highest = lax.Precision.HIGHEST
    score_scale = 2.0 / math.sqrt(source.shape[1])
    source_f32 = source.astype(jnp.float32)
    target_f32 = target.astype(jnp.float32)
    current = start_map
    for iteration in range(ITERS):
        mapped = jnp.dot(
            source, current.astype(jnp.bfloat16), preferred_element_type=jnp.float32
        ).astype(jnp.bfloat16)
        scores = (
            lax.dot_general(
                mapped, target, (((1,), (1,)), ((), ())), preferred_element_type=jnp.float32
            )
            * score_scale
        )
        row_local = jnp.max(scores, axis=1)
        col_local = jnp.max(scores, axis=0)
        row_part = jnp.sum(jnp.exp(scores - row_local[:, None]), axis=1)
        col_part = jnp.sum(jnp.exp(scores - col_local[None, :]), axis=0)
        row_top, row_total, col_top, col_total = gather_stats(row_local, row_part, col_local, col_part)
        row_weights = (jnp.exp(scores - row_top[:, None]) / row_total[:, None]).astype(jnp.bfloat16)
        col_weights = (jnp.exp(scores - col_top[None, :]) / col_total[None, :]).astype(jnp.bfloat16)
        source_part = jnp.dot(row_weights, target, preferred_element_type=jnp.float32)
        target_part = lax.dot_general(
            col_weights, source, (((0,), (0,)), ((), ())), preferred_element_type=jnp.float32
        )
        source_hi = source_part.astype(jnp.bfloat16)
        source_lo = (source_part - source_hi.astype(jnp.float32)).astype(jnp.bfloat16)
        target_hi = target_part.astype(jnp.bfloat16)
        target_lo = (target_part - target_hi.astype(jnp.float32)).astype(jnp.bfloat16)
        down = (((0,), (0,)), ((), ()))
        covariance = (
            lax.dot_general(source, source_hi, down, preferred_element_type=jnp.float32)
            + lax.dot_general(source, source_lo, down, preferred_element_type=jnp.float32)
            + lax.dot_general(target_hi, target, down, preferred_element_type=jnp.float32)
            + lax.dot_general(target_lo, target, down, preferred_element_type=jnp.float32)
        )
        if iteration == ITERS - 1:
            covariance, target_soft, source_soft = all_reduce(covariance, target_part, source_part)
        else:
            covariance = all_reduce(covariance)
        current = polar_steps(covariance)
    return (source_soft, target_soft, current)


def solution(mesh):
    in_specs = (P("src", None), P("tgt", None), P())
    out_specs = (P(("src", "tgt"), None), P("tgt", None), P())
    return jax.shard_map(body, mesh=mesh, in_specs=in_specs, out_specs=out_specs, check_vma=False)
```
